512 devices in a mesh: pts: 64 (over z, y), freq: 8 (over x, core).
Axes of the slice: x: 4, y: 8, z: 8, core: 2. Of those that a mesh axis runs over, the one named last changes fastest.
Arguments:
- snapshots: float32 [2112, 196608], P(None, ('pts', 'freq')), may hold values from -6 to 6
- weight: float32 [196608], P('pts'), may hold values from 0.1 to 10
- start_vec: float32 [64, 2, 32], replicated, may hold values from -6 to 6
Outputs:
- gram_mine: float32 [64, 2, 32, 32], P('freq')
- modes: float32 [64, 2, 196608], P('freq', None, 'pts')
The draws below stay inside these ranges and needn't reach their ends.
All inputs are finite; a program needn't handle non-finite values.
Results may differ from the reference program's by a relative error of at most 0.0003.
Values sent between devices are 32-bit elements; how exact they have to be, the bound alone decides.
A program may use at most 64 MiB of HBM per device.

```python
import math
import jax
import jax.numpy as jnp
from jax import lax

NFFT = 128
NB = 32
NF = 64
ROWS = 196608
TIMES = 2112
N_PTS = 64


def draw_snapshots(key, part):
    key_offset = jax.random.fold_in(key, 11)
    key_noise = jax.random.fold_in(key, 23)
    offset = jax.random.uniform(key_offset, (1, ROWS), jnp.float32, -2.0, 2.0)
    fluct_part = jnp.clip(jax.random.normal(key_noise, (TIMES, ROWS), jnp.float32), -3.5, 3.5)
    return (offset + fluct_part).astype(jnp.float32)


def block_scale(own_key, dims, cuts, smallest, top_value):
    level = 1.0
    for position, parts in cuts:
        draws = jax.random.uniform(jax.random.fold_in(jax.random.fold_in(own_key, 6), position), (parts,), jnp.float32, smallest / len(cuts), top_value / len(cuts))
        level = level * jnp.repeat(jnp.exp(draws), dims[position] // parts).reshape((-1,) + (1,) * (len(dims) - 1 - position))
    return level


def bell_draw(key, extent, deviation, reach, kind=jnp.bfloat16):
    return jnp.clip(deviation * jax.random.normal(key, extent, jnp.float32), -reach, reach).astype(kind)


def setup_inputs(seed: int = 0) -> dict:
    seeds = jax.random.split(jax.random.key(seed), 4)
    snapshots = draw_snapshots(jax.random.fold_in(seeds[3], 71), 0)
    weight = jnp.clip(jnp.exp(math.log(10.0) - 4.6051702 * jax.random.uniform(seeds[1], (ROWS,), jnp.float32) ** block_scale(seeds[1], (ROWS,), ((0, 64),), -0.2, 0.2)), 0.1, 10.0)
    start_vec = bell_draw(seeds[2], (NF, 2, NB), 1.0, 6.0, jnp.float32)
    return dict(snapshots=snapshots, weight=weight, start_vec=start_vec)


def dft_table():
    times = jnp.arange(NFFT, dtype=jnp.int32)
    freqs = jnp.arange(NF, dtype=jnp.int32)
    phases = (freqs[:, None] * times[None, :] % NFFT).astype(jnp.float32) * (2.0 * math.pi / NFFT)
    window = 0.5 - 0.5 * jnp.cos(times.astype(jnp.float32) * (2.0 * math.pi / NFFT))
    weighted = window / jnp.sqrt(jnp.sum(window * window))
    return jnp.stack([jnp.cos(phases) * weighted, -jnp.sin(phases) * weighted], axis=1)

def spectra_of(block, dft_rows):
    fluct_rows = block - lax.optimization_barrier(jnp.mean(block, axis=0, keepdims=True))
    halves = fluct_rows.reshape(NB + 1, NFFT // 2, block.shape[1])
    early = jnp.einsum('kct,btr->kcbr', dft_rows[:, :, :NFFT // 2], halves[:-1], precision=lax.Precision.HIGHEST)
    later = jnp.einsum('kct,btr->kcbr', dft_rows[:, :, NFFT // 2:], halves[1:], precision=lax.Precision.HIGHEST)
    return early + later

def gram_of(spectra, weight, total_rows):
    real_part = spectra[:, 0]
    imag_part = spectra[:, 1]
    real_w = real_part * weight
    imag_w = imag_part * weight
    gram_real = jnp.einsum('fjr,fkr->fjk', real_w, real_part, precision=lax.Precision.HIGHEST) + jnp.einsum('fjr,fkr->fjk', imag_w, imag_part, precision=lax.Precision.HIGHEST)
    gram_imag = jnp.einsum('fjr,fkr->fjk', real_w, imag_part, precision=lax.Precision.HIGHEST) - jnp.einsum('fjr,fkr->fjk', imag_w, real_part, precision=lax.Precision.HIGHEST)
    return jnp.stack([gram_real, gram_imag], axis=1) / total_rows

def response_of(gram, start_vec):
    resp_real = jnp.einsum('fjk,fk->fj', gram[:, 0], start_vec[:, 0], precision=lax.Precision.HIGHEST) - jnp.einsum('fjk,fk->fj', gram[:, 1], start_vec[:, 1], precision=lax.Precision.HIGHEST)
    resp_imag = jnp.einsum('fjk,fk->fj', gram[:, 0], start_vec[:, 1], precision=lax.Precision.HIGHEST) + jnp.einsum('fjk,fk->fj', gram[:, 1], start_vec[:, 0], precision=lax.Precision.HIGHEST)
    scaling = 1.0 / jnp.sqrt(lax.optimization_barrier(jnp.mean(resp_real * resp_real + resp_imag * resp_imag, axis=1, keepdims=True)) + 1e-06)
    return jnp.stack([resp_real * scaling, resp_imag * scaling], axis=1)

def project(spectra, response):
    real_part = spectra[:, 0]
    imag_part = spectra[:, 1]
    mode_real = jnp.einsum('fjr,fj->fr', real_part, response[:, 0], precision=lax.Precision.HIGHEST) - jnp.einsum('fjr,fj->fr', imag_part, response[:, 1], precision=lax.Precision.HIGHEST)
    mode_imag = jnp.einsum('fjr,fj->fr', real_part, response[:, 1], precision=lax.Precision.HIGHEST) + jnp.einsum('fjr,fj->fr', imag_part, response[:, 0], precision=lax.Precision.HIGHEST)
    return jnp.stack([mode_real, mode_imag], axis=1)

def reference(snapshots, weight, start_vec):
    dft_rows = dft_table()
    block_rows = ROWS // N_PTS
    indices = jnp.arange(N_PTS, dtype=jnp.int32)

    def block_gram(index):
        first = (index * block_rows).astype(jnp.int32)
        block = lax.dynamic_slice_in_dim(snapshots, first, block_rows, 1)
        weights_block = lax.dynamic_slice_in_dim(weight, first, block_rows, 0)
        return gram_of(spectra_of(block, dft_rows), weights_block, ROWS)
    gram_full = lax.optimization_barrier(jnp.sum(lax.map(block_gram, indices), axis=0))
    response = response_of(gram_full, start_vec)

    def block_modes(index):
        first = (index * block_rows).astype(jnp.int32)
        block = lax.dynamic_slice_in_dim(snapshots, first, block_rows, 1)
        return project(spectra_of(block, dft_rows), response)
    pieces = lax.map(block_modes, indices)
    modes = jnp.transpose(pieces, (1, 2, 0, 3)).reshape(NF, 2, ROWS)
    return (gram_full, modes)
```

```python
import functools
import math

import jax
import jax.numpy as jnp
import numpy as np
from jax import lax
from jax.experimental import pallas as pl
from jax.experimental.pallas import tpu as pltpu
from jax.sharding import PartitionSpec as P

NFFT = 128
NB = 32
NF = 64
HALF = NFFT // 2
NC = 8
NY = 8
MESH = pl.DeviceIdType.MESH
BF = jnp.bfloat16
F32 = jnp.float32


def dft_operand():
    times = np.arange(NFFT)
    phases = (np.arange(NF)[:, None] * times[None, :] % NFFT) * (2.0 * math.pi / NFFT)
    window = 0.5 - 0.5 * np.cos(times * (2.0 * math.pi / NFFT))
    window = window / np.sqrt(np.sum(window * window))
    rows = np.stack([np.cos(phases) * window, -np.sin(phases) * window], axis=1)
    rows = rows.reshape(2 * NF, NFFT).astype(np.float32)
    high = rows.astype(BF)
    low = (rows - high.astype(np.float32)).astype(BF)
    zero = np.zeros_like(low[:, :HALF])
    top = np.concatenate([high[:, :HALF], high[:, :HALF], high[:, HALF:], high[:, HALF:]], axis=1)
    bottom = np.concatenate([low[:, :HALF], zero, low[:, HALF:], zero], axis=1)
    return np.concatenate([top, bottom], axis=0)


def split(value):
    high = value.astype(BF)
    return high, (value - high.astype(F32)).astype(BF)


def dot(a, b):
    return lax.dot_general(a, b, (((1,), (0,)), ((), ())), preferred_element_type=F32)


def dot_t(a, b):
    return lax.dot_general(a, b, (((1,), (1,)), ((), ())), preferred_element_type=F32)


def lanes(shape, axis=1):
    return lax.broadcasted_iota(jnp.int32, shape, axis)


def kernel(
    nz,
    total_rows,
    snap_hbm,
    weight_ref,
    start_ref,
    table_ref,
    gram_out,
    modes_out,
    x_ref,
    xc_ref,
    q_ref,
    ah_ref,
    al_ref,
    gs_ref,
    gr_ref,
    gx_ref,
    gy_ref,
    gz_ref,
    gf_ref,
    vy_ref,
    vz_ref,
    e_ref,
    ms_ref,
    mr_ref,
    sa_ref,
    sb_ref,
    load_sem,
    gx_s,
    gx_r,
    gy_s,
    gy_r,
    gz_s,
    gz_r,
    ga_s,
    ga_r,
    vy_s,
    vy_r,
    vz_s,
    vz_r,
    e_s,
    e_r,
    m_s,
    m_r,
):
    halves = x_ref.shape[0] // HALF
    rows = x_ref.shape[1]
    pts = lax.axis_index("pts")
    me = lax.axis_index("freq")
    zc = pts // NY
    yc = pts % NY
    xc = me // 2
    core = me % 2

    chunks = load_sem.shape[0]
    span = x_ref.shape[0] // chunks

    def load(i):
        part = pl.ds(i * span, span)
        return pltpu.make_async_copy(snap_hbm.at[part, :], x_ref.at[part, :], load_sem.at[i])

    for i in range(chunks):
        load(i).start()

    def freq_peer(i):
        return ((xc + 3 - i // 2) % (NC // 2)) * 2 + (core + 1 - i % 2) % 2

    barrier = pltpu.get_barrier_semaphore()
    for i in range(NC - 1):
        pl.semaphore_signal(barrier, inc=1, device_id={"freq": freq_peer(i)}, device_id_type=MESH)
    for d in range(1, NY):
        pl.semaphore_signal(
            barrier, inc=1, device_id={"pts": zc * NY + (yc + d) % NY}, device_id_type=MESH
        )
    for d in range(1, nz):
        pl.semaphore_signal(
            barrier, inc=1, device_id={"pts": (zc + d) % nz * NY + yc}, device_id_type=MESH
        )

    groups = rows // 128
    weight = jnp.concatenate(
        [weight_ref[pl.ds(me * groups + j, 1), :] for j in range(groups)], axis=1
    )
    root = jnp.sqrt(weight)
    inv_root = 1.0 / root
    eye = lanes((NB, NB), 0) == lanes((NB, NB), 1)

    def column(k, c):
        row = start_ref[me * (NF // NC) + k, pl.ds(c, 1), :]
        col = jnp.sum(jnp.where(eye, row, 0.0), axis=1, keepdims=True)
        return jnp.broadcast_to(col, (NB, 128))

    seg = lanes((NB, 128)) // 32
    for p in range(NF // NC // 2):
        r1, i1 = column(2 * p, 0), column(2 * p, 1)
        r2, i2 = column(2 * p + 1, 0), column(2 * p + 1, 1)
        sa_ref[p] = jnp.where(seg == 0, r1, jnp.where(seg == 1, r2, jnp.where(seg == 2, i1, i2)))
        sb_ref[p] = jnp.where(seg == 0, i1, jnp.where(seg == 1, i2, jnp.where(seg == 2, -r1, -r2)))

    total = jnp.zeros((24, rows), F32)
    for i in range(chunks):
        load(i).wait()
        for j in range(span // 24):
            total = total + x_ref[i * span + j * 24 : i * span + (j + 1) * 24, :]
    mean = jnp.sum(total, axis=0, keepdims=True) * (1.0 / x_ref.shape[0])

    def centre(j):
        high, low = split(x_ref[pl.ds(pl.multiple_of(j * HALF, HALF), HALF), :] - mean)
        xc_ref[pl.ds(pl.multiple_of(j * NFFT, NFFT), HALF), :] = high
        xc_ref[pl.ds(pl.multiple_of(j * NFFT + HALF, HALF), HALF), :] = low

    centre(0)
    centre(1)

    def transform(b, carry):
        both = dot(table_ref[...], xc_ref[pl.ds(pl.multiple_of(b * NFFT, NFFT), 2 * NFFT), :])
        value = (both[: 2 * NF] + both[2 * NF :]) * root
        for j in range(groups):
            q_ref[j, pl.ds(b, 2 * NF, stride=NB), :] = value[:, j * 128 : (j + 1) * 128]
        centre(jnp.minimum(b + 2, halves - 1))
        return carry

    lax.fori_loop(0, NB, transform, 0)

    pl.semaphore_wait(barrier, NC - 1 + NY - 1 + nz - 1)

    per = NF // NC
    block = per * 2 * NB

    def gram_copy(to, slot):
        return pltpu.make_async_remote_copy(
            src_ref=gs_ref.at[to],
            dst_ref=gr_ref.at[slot],
            send_sem=gx_s.at[to],
            recv_sem=gx_r.at[slot],
            device_id={"freq": to},
            device_id_type=MESH,
        )

    def gram_of(owner):
        for p in range(per // 2):
            first = pl.multiple_of(owner * block + p * 128, 128)
            value = [q_ref[j, pl.ds(first, 128), :] for j in range(groups)]
            high, low = split(jnp.concatenate(value, axis=1))
            ah_ref[pl.ds(first, 128), :] = high
            al_ref[pl.ds(first, 128), :] = low

            def reim(v):
                return (
                    jnp.concatenate([v[0:32], v[64:96]], axis=0),
                    jnp.concatenate([v[32:64], v[96:128]], axis=0),
                )

            rh, ih = reim(high)
            rl, il = reim(low)
            h1 = jnp.concatenate([rh, ih], axis=1)
            l1 = jnp.concatenate([rl, il], axis=1)
            h2 = jnp.concatenate([ih, -rh], axis=1)
            l2 = jnp.concatenate([il, -rl], axis=1)
            out = dot_t(
                jnp.concatenate([h1, l1], axis=0), jnp.concatenate([h1, h2, l1, l2], axis=0)
            )
            z = out[0:64, 0:128] + (out[0:64, 128:256] + out[64:128, 0:128])
            gs_ref[owner, pl.ds(p * NB, NB), :] = jnp.where(seg % 2 == 0, z[0:32], z[32:64])

    def gram_step(i, carry):
        owner = freq_peer(i)
        gram_of(owner)
        gram_copy(owner, me).start()
        return carry

    lax.fori_loop(0, NC - 1, gram_step, 0)
    gram_of(me)

    gx_ref[...] = gs_ref[me]

    def gram_sum(i, carry):
        sender = ((xc + 1 + i // 2) % (NC // 2)) * 2 + (core + 1 - i % 2) % 2
        gram_copy(sender, sender).wait_recv()
        gx_ref[...] += gr_ref[sender]
        return carry

    lax.fori_loop(0, NC - 1, gram_sum, 0)

    parts_a, parts_b = [], []
    for p in range(per // 2):
        g = gx_ref[p * NB : (p + 1) * NB, :]
        parts_a.append(jnp.sum(g * sa_ref[p], axis=0, keepdims=True))
        parts_b.append(jnp.sum(g * sb_ref[p], axis=0, keepdims=True))
    vy_ref[yc] = jnp.concatenate(parts_a + parts_b, axis=0)

    gsub = gx_ref.shape[0] // NY

    def y_dev(other):
        return {"pts": zc * NY + other}

    def z_dev(other):
        return {"pts": other * NY + yc}

    def spread(buf, ssem, rsem, mine, other, device):
        return pltpu.make_async_remote_copy(
            src_ref=buf.at[mine],
            dst_ref=buf.at[mine],
            send_sem=ssem.at[other],
            recv_sem=rsem.at[mine],
            device_id=device,
            device_id_type=MESH,
        )

    def arrival(buf, ssem, rsem, other, device):
        return pltpu.make_async_remote_copy(
            src_ref=buf.at[other],
            dst_ref=buf.at[other],
            send_sem=ssem.at[other],
            recv_sem=rsem.at[other],
            device_id=device,
            device_id_type=MESH,
        )

    def total_of(buf, n):
        out = buf[0]
        for i in range(1, n):
            out = out + buf[i]
        return out

    for d in range(1, NY):
        other = (yc + d) % NY
        spread(vy_ref, vy_s, vy_r, yc, other, y_dev(other)).start()

    def gram_y(other, slot):
        return pltpu.make_async_remote_copy(
            src_ref=gx_ref.at[pl.ds(pl.multiple_of(other * gsub, gsub), gsub), :],
            dst_ref=gy_ref.at[slot],
            send_sem=gy_s.at[other],
            recv_sem=gy_r.at[slot],
            device_id=y_dev(other),
            device_id_type=MESH,
        )

    for d in range(1, NY):
        gram_y((yc + d) % NY, yc).start()
    gy_ref[yc] = gx_ref[pl.ds(pl.multiple_of(yc * gsub, gsub), gsub), :]

    for d in range(1, NY):
        other = (yc + d) % NY
        arrival(vy_ref, vy_s, vy_r, other, y_dev(other)).wait_recv()
    vz_ref[zc] = total_of(vy_ref, NY)
    for d in range(1, nz):
        other = (zc + d) % nz
        spread(vz_ref, vz_s, vz_r, zc, other, z_dev(other)).start()

    for d in range(1, NY):
        other = (yc + d) % NY
        gram_y(other, other).wait_recv()
    gz_ref[zc] = total_of(gy_ref, NY)
    for d in range(1, nz):
        other = (zc + d) % nz
        spread(gz_ref, gz_s, gz_r, zc, other, z_dev(other)).start()

    for d in range(1, nz):
        other = (zc + d) % nz
        arrival(vz_ref, vz_s, vz_r, other, z_dev(other)).wait_recv()
    v = total_of(vz_ref, nz) * (1.0 / total_rows)

    lane = lanes((per // 2, 128))
    odd = (lane // 32) % 2 == 1
    va, vb = v[0 : per // 2], v[per // 2 :]
    vr = va + pltpu.roll(va, 64, 1)
    vi = vb + pltpu.roll(vb, 64, 1)
    square = vr * vr + vi * vi
    norm1 = jnp.sum(jnp.where(lane < 32, square, 0.0), axis=1, keepdims=True) * (1.0 / NB)
    norm2 = jnp.sum(jnp.where((lane >= 32) & (lane < 64), square, 0.0), axis=1, keepdims=True)
    norm2 = norm2 * (1.0 / NB)
    scale = jnp.where(odd, 1.0 / jnp.sqrt(norm2 + 1e-06), 1.0 / jnp.sqrt(norm1 + 1e-06))
    yr = vr * scale
    yi = vi * scale
    k1re = jnp.where(odd, -pltpu.roll(yi, 32, 1), yr)
    k1im = jnp.where(odd, pltpu.roll(yr, 32, 1), yi)
    k2re = jnp.where(odd, -yi, pltpu.roll(yr, 96, 1))
    k2im = jnp.where(odd, yr, pltpu.roll(yi, 96, 1))
    pieces = []
    for p in range(per // 2):
        pieces += [w[p : p + 1] for w in (k1re, k1im, k2re, k2im)]
    e_ref[me] = jnp.concatenate(pieces, axis=0)

    def e_send(i, carry):
        to = freq_peer(i)
        spread(e_ref, e_s, e_r, me, to, {"freq": to}).start()
        return carry

    lax.fori_loop(0, NC - 1, e_send, 0)

    own = lanes((2 * per, block)) // 64 == lanes((2 * per, block), 0) // 2

    def project(owner):
        e = e_ref[owner]
        left = jnp.where(own, jnp.concatenate([e] * (block // 128), axis=1), 0.0)
        high, low = split(left)
        first = pl.multiple_of(owner * block, block)
        right = ah_ref[pl.ds(first, block), :]
        both = dot(jnp.concatenate([high, low], axis=0), right)
        out = both[: 2 * per] + both[2 * per :] + dot(high, al_ref[pl.ds(first, block), :])
        return out * inv_root

    mr_ref[me] = project(me)

    for d in range(1, nz):
        other = (zc + d) % nz
        arrival(gz_ref, gz_s, gz_r, other, z_dev(other)).wait_recv()
    gf_ref[yc] = total_of(gz_ref, nz) * (1.0 / total_rows)
    for d in range(1, NY):
        other = (yc + d) % NY
        spread(gf_ref, ga_s, ga_r, yc, other, y_dev(other)).start()

    def modes_copy(to, slot):
        return pltpu.make_async_remote_copy(
            src_ref=ms_ref.at[to],
            dst_ref=mr_ref.at[slot],
            send_sem=m_s.at[to],
            recv_sem=m_r.at[slot],
            device_id={"freq": to},
            device_id_type=MESH,
        )

    def mode_step(i, carry):
        owner = freq_peer(i)
        arrival(e_ref, e_s, e_r, owner, {"freq": owner}).wait_recv()
        ms_ref[owner] = project(owner)
        modes_copy(owner, me).start()
        return carry

    lax.fori_loop(0, NC - 1, mode_step, 0)

    for d in range(1, NY):
        other = (yc + d) % NY
        arrival(gf_ref, ga_s, ga_r, other, y_dev(other)).wait_recv()
    for p in range(per // 2):
        step = NB // gsub
        g = jnp.concatenate([gf_ref[p * step + j] for j in range(step)], axis=0)
        for k in range(2):
            for c in range(2):
                row = ((2 * p + k) * 2 + c) * NB
                shift = (128 - (c * 64 + k * 32)) % 128
                turned = g if shift == 0 else pltpu.roll(g, shift, 1)
                gram_out[row : row + NB, :] = turned[:, :NB]

    def modes_wait(i, carry):
        sender = freq_peer(i)
        modes_copy(sender, sender).wait_recv()
        return carry

    lax.fori_loop(0, NC - 1, modes_wait, 0)
    for s in range(NC):
        modes_out[:, s * rows : (s + 1) * rows] = mr_ref[s]

    def sent_x(i, carry):
        to = freq_peer(i)
        gram_copy(to, me).wait_send()
        spread(e_ref, e_s, e_r, me, to, {"freq": to}).wait_send()
        modes_copy(to, me).wait_send()
        return carry

    lax.fori_loop(0, NC - 1, sent_x, 0)
    for d in range(1, NY):
        other = (yc + d) % NY
        spread(vy_ref, vy_s, vy_r, yc, other, y_dev(other)).wait_send()
        gram_y(other, yc).wait_send()
        spread(gf_ref, ga_s, ga_r, yc, other, y_dev(other)).wait_send()
    for d in range(1, nz):
        other = (zc + d) % nz
        spread(vz_ref, vz_s, vz_r, zc, other, z_dev(other)).wait_send()
        spread(gz_ref, gz_s, gz_r, zc, other, z_dev(other)).wait_send()


def shards(nz, table, snapshots, weight, start_vec):
    times, rows = snapshots.shape
    total_rows = weight.shape[0] * lax.axis_size("pts")
    per = NF // NC
    dma = pltpu.SemaphoreType.DMA
    vmem = pl.BlockSpec(memory_space=pltpu.VMEM)
    gram_rows = per // 2 * NB
    gram, modes = pl.pallas_call(
        functools.partial(kernel, nz, total_rows),
        out_shape=(
            jax.ShapeDtypeStruct((per * 2 * NB, NB), F32),
            jax.ShapeDtypeStruct((per * 2, NC * rows), F32),
        ),
        in_specs=[pl.BlockSpec(memory_space=pl.ANY), vmem, vmem, vmem],
        out_specs=(vmem, vmem),
        scratch_shapes=[
            pltpu.VMEM((times, rows), F32),
            pltpu.VMEM((times * 2, rows), BF),
            pltpu.VMEM((rows // 128, NF * 2 * NB, 128), F32),
            pltpu.VMEM((NF * 2 * NB, rows), BF),
            pltpu.VMEM((NF * 2 * NB, rows), BF),
            pltpu.VMEM((NC, gram_rows, 128), F32),
            pltpu.VMEM((NC, gram_rows, 128), F32),
            pltpu.VMEM((gram_rows, 128), F32),
            pltpu.VMEM((NY, gram_rows // NY, 128), F32),
            pltpu.VMEM((nz, gram_rows // NY, 128), F32),
            pltpu.VMEM((NY, gram_rows // NY, 128), F32),
            pltpu.VMEM((NY, per, 128), F32),
            pltpu.VMEM((nz, per, 128), F32),
            pltpu.VMEM((NC, per * 2, 128), F32),
            pltpu.VMEM((NC, per * 2, rows), F32),
            pltpu.VMEM((NC, per * 2, rows), F32),
            pltpu.VMEM((per // 2, NB, 128), F32),
            pltpu.VMEM((per // 2, NB, 128), F32),
            dma((8,)),
            dma((NC,)),
            dma((NC,)),
            dma((NY,)),
            dma((NY,)),
            dma((nz,)),
            dma((nz,)),
            dma((NY,)),
            dma((NY,)),
            dma((NY,)),
            dma((NY,)),
            dma((nz,)),
            dma((nz,)),
            dma((NC,)),
            dma((NC,)),
            dma((NC,)),
            dma((NC,)),
        ],
        compiler_params=pltpu.CompilerParams(collective_id=0, has_side_effects=True),
        name="spod",
    )(snapshots, weight.reshape(-1, 128), start_vec, table)
    return gram.reshape(per, 2, NB, NB), modes.reshape(per, 2, NC * rows)


def solution(mesh):
    placed = (P(None, ("pts", "freq")), P("pts"), P())
    nz = mesh.shape["pts"] // NY
    return jax.shard_map(
        functools.partial(shards, nz, dft_operand()),
        mesh=mesh,
        in_specs=placed,
        out_specs=(P("freq", None, None, None), P("freq", None, "pts")),
        check_vma=False,
    )
```

```python
import functools
import math

import jax
import jax.numpy as jnp
import numpy as np
from jax import lax
from jax.experimental import pallas as pl
from jax.experimental.pallas import tpu as pltpu
from jax.sharding import PartitionSpec as P

NFFT = 128
NB = 32
NF = 64
HALF = NFFT // 2
NC = 8
NY = 8
PITCH = NB + 1
MESH = pl.DeviceIdType.MESH
BF = jnp.bfloat16
F32 = jnp.float32


def dft_operand():
    times = np.arange(NFFT)
    phases = (np.arange(NF)[:, None] * times[None, :] % NFFT) * (2.0 * math.pi / NFFT)
    window = 0.5 - 0.5 * np.cos(times * (2.0 * math.pi / NFFT))
    window = window / np.sqrt(np.sum(window * window))
    rows = np.stack([np.cos(phases) * window, -np.sin(phases) * window], axis=1)
    rows = rows.reshape(2 * NF, NFFT).astype(np.float32)
    high = rows.astype(BF)
    low = (rows - high.astype(np.float32)).astype(BF)
    zero = np.zeros_like(low[:, :HALF])
    top = np.concatenate([high[:, :HALF], high[:, :HALF], high[:, HALF:], high[:, HALF:]], axis=1)
    bottom = np.concatenate([low[:, :HALF], zero, low[:, HALF:], zero], axis=1)
    return np.concatenate([top, bottom], axis=0)


def split(value):
    high = value.astype(BF)
    return high, (value - high.astype(F32)).astype(BF)


def dot(a, b):
    return lax.dot_general(a, b, (((1,), (0,)), ((), ())), preferred_element_type=F32)


def dot_t(a, b):
    return lax.dot_general(a, b, (((1,), (1,)), ((), ())), preferred_element_type=F32)


def lanes(shape, axis=1):
    return lax.broadcasted_iota(jnp.int32, shape, axis)


def kernel(
    nz,
    total_rows,
    snap_hbm,
    weight_ref,
    start_ref,
    table_ref,
    gram_out,
    modes_out,
    x_ref,
    xc_ref,
    q_ref,
    ah_ref,
    al_ref,
    gs_ref,
    gr_ref,
    vs_ref,
    vx_ref,
    gx_ref,
    gy_ref,
    gz_ref,
    gf_ref,
    vy_ref,
    vz_ref,
    e_ref,
    ms_ref,
    mr_ref,
    sa_ref,
    sb_ref,
    load_sem,
    gx_s,
    gx_r,
    gy_s,
    gy_r,
    gz_s,
    gz_r,
    ga_s,
    ga_r,
    vx_s,
    vx_r,
    vy_s,
    vy_r,
    vz_s,
    vz_r,
    e_s,
    e_r,
    m_s,
    m_r,
):
    halves = x_ref.shape[0] // HALF
    rows = x_ref.shape[1]
    pts = lax.axis_index("pts")
    me = lax.axis_index("freq")
    zc = pts // NY
    yc = pts % NY
    xc = me // 2
    core = me % 2

    chunks = load_sem.shape[0]
    span = x_ref.shape[0] // chunks

    def load(i):
        part = pl.ds(i * span, span)
        return pltpu.make_async_copy(snap_hbm.at[part, :], x_ref.at[part, :], load_sem.at[i])

    for i in range(chunks):
        load(i).start()

    def freq_peer(i):
        return ((xc + 3 - i // 2) % (NC // 2)) * 2 + (core + 1 - i % 2) % 2

    barrier = pltpu.get_barrier_semaphore()
    for i in range(NC - 1):
        pl.semaphore_signal(barrier, inc=1, device_id={"freq": freq_peer(i)}, device_id_type=MESH)
    for d in range(1, NY):
        pl.semaphore_signal(
            barrier, inc=1, device_id={"pts": zc * NY + (yc + d) % NY}, device_id_type=MESH
        )
    for d in range(1, nz):
        pl.semaphore_signal(
            barrier, inc=1, device_id={"pts": (zc + d) % nz * NY + yc}, device_id_type=MESH
        )

    groups = rows // 128
    weight = jnp.concatenate(
        [weight_ref[pl.ds(me * groups + j, 1), :] for j in range(groups)], axis=1
    )
    root = jnp.sqrt(weight)
    inv_root = 1.0 / root
    seg = lanes((NB, 128)) // 32
    coeffs = jnp.concatenate([start_ref[0], start_ref[1]], axis=1)

    def tables(i, carry):
        turned = pltpu.roll(coeffs, 128 - 4 * i, 1)
        for odd in range(2):
            r1, r2, i1, i2 = (
                jnp.broadcast_to(turned[:, n : n + 1], (NB, 128))
                for n in (2 * odd, 2 * odd + 1, 64 + 2 * odd, 65 + 2 * odd)
            )
            at = seg if odd == 0 else (seg + 2) % 4
            pair = 2 * i + odd
            sa_ref[pair] = jnp.where(at == 0, r1, jnp.where(at == 1, r2, jnp.where(at == 2, i1, i2)))
            sb_ref[pair] = jnp.where(at == 0, i1, jnp.where(at == 1, i2, jnp.where(at == 2, -r1, -r2)))
        return carry

    lax.fori_loop(0, NF // 4, tables, 0)

    total = jnp.zeros((24, rows), F32)
    for i in range(chunks):
        load(i).wait()
        for j in range(span // 24):
            total = total + x_ref[i * span + j * 24 : i * span + (j + 1) * 24, :]
    mean = jnp.sum(total, axis=0, keepdims=True) * (1.0 / x_ref.shape[0])

    def centre(j):
        high, low = split((x_ref[pl.ds(pl.multiple_of(j * HALF, HALF), HALF), :] - mean) * root)
        xc_ref[pl.ds(pl.multiple_of(j * NFFT, NFFT), HALF), :] = high
        xc_ref[pl.ds(pl.multiple_of(j * NFFT + HALF, HALF), HALF), :] = low

    centre(0)
    centre(1)

    def transform(b, carry):
        both = dot(table_ref[...], xc_ref[pl.ds(pl.multiple_of(b * NFFT, NFFT), 2 * NFFT), :])
        value = both[: 2 * NF] + both[2 * NF :]
        for j in range(groups):
            q_ref[j, pl.ds(b, 2 * NF, stride=PITCH), :] = value[:, j * 128 : (j + 1) * 128]
        centre(jnp.minimum(b + 2, halves - 1))
        return carry

    lax.fori_loop(0, NB, transform, 0)

    pl.semaphore_wait(barrier, NC - 1 + NY - 1 + nz - 1)

    per = NF // NC
    block = per * 2 * NB

    def gram_copy(to, slot):
        return pltpu.make_async_remote_copy(
            src_ref=gs_ref.at[to],
            dst_ref=gr_ref.at[slot],
            send_sem=gx_s.at[to],
            recv_sem=gx_r.at[slot],
            device_id={"freq": to},
            device_id_type=MESH,
        )

    def vx_copy(to, slot):
        return pltpu.make_async_remote_copy(
            src_ref=vs_ref.at[to],
            dst_ref=vx_ref.at[slot],
            send_sem=vx_s.at[to],
            recv_sem=vx_r.at[slot],
            device_id={"freq": to},
            device_id_type=MESH,
        )

    upper = lanes((NB, 128), 0) <= lanes((NB, 128)) % 32
    lane4 = lanes((per // 2, 128))
    lane = lanes((NB, 128))

    def gram_of(owner):
        parts_a, parts_b, packed = [], [], None
        for p in range(per // 2):
            first = pl.multiple_of(owner * block + p * 128, 128)
            for n in range(4):
                source = (owner * (2 * per) + p * 4 + n) * PITCH
                value = [q_ref[j, pl.ds(source, NB), :] for j in range(groups)]
                high, low = split(jnp.concatenate(value, axis=1))
                ah_ref[pl.ds(first + n * NB, NB), :] = high
                al_ref[pl.ds(first + n * NB, NB), :] = low

            def reim(ref):
                v = [ref[pl.ds(first + n * NB, NB), :] for n in range(4)]
                return jnp.concatenate([v[0], v[2]], axis=0), jnp.concatenate([v[1], v[3]], axis=0)

            rh, ih = reim(ah_ref)
            rl, il = reim(al_ref)
            h1 = jnp.concatenate([rh, ih], axis=1)
            l1 = jnp.concatenate([rl, il], axis=1)
            h2 = jnp.concatenate([ih, -rh], axis=1)
            l2 = jnp.concatenate([il, -rl], axis=1)
            right = [h1, h2, l1, l2] if p % 2 == 0 else [h2, h1, l2, l1]
            out = dot_t(jnp.concatenate([h1, l1], axis=0), jnp.concatenate(right, axis=0))
            z = out[0:64, 0:128] + (out[0:64, 128:256] + out[64:128, 0:128])
            g = jnp.where(seg % 2 == 0, z[0:32], z[32:64])
            pair = owner * (per // 2) + p
            parts_a.append(jnp.sum(g * sa_ref[pair], axis=0, keepdims=True))
            parts_b.append(jnp.sum(g * sb_ref[pair], axis=0, keepdims=True))
            half = jnp.where(upper, g, pltpu.roll(g, 64, 1))
            if p % 2 == 0:
                packed = half
            else:
                both = jnp.where(lane < 64, packed, half)
                gs_ref[owner, pl.ds(p // 2 * NB, NB), :] = both
        va = jnp.concatenate(parts_a, axis=0)
        vb = jnp.concatenate(parts_b, axis=0)
        vs_ref[owner] = jnp.where(
            lane4 < 64, va + pltpu.roll(va, 64, 1), vb + pltpu.roll(vb, 64, 1)
        )

    def gram_step(i, carry):
        owner = freq_peer(i)
        gram_of(owner)
        vx_copy(owner, me).start()
        gram_copy(owner, me).start()
        return carry

    lax.fori_loop(0, NC - 1, gram_step, 0)
    gram_of(me)
    vx_ref[me] = vs_ref[me]
    gr_ref[me] = gs_ref[me]

    def total_of(buf, n):
        out = buf[0]
        for i in range(1, n):
            out = out + buf[i]
        return out

    for i in range(NC - 1):
        sender = freq_peer(i)
        vx_copy(sender, sender).wait_recv()
    vy_ref[yc] = total_of(vx_ref, NC)

    gsub = gx_ref.shape[0] // NY

    def y_dev(other):
        return {"pts": zc * NY + other}

    def z_dev(other):
        return {"pts": other * NY + yc}

    def spread(buf, ssem, rsem, mine, other, device):
        return pltpu.make_async_remote_copy(
            src_ref=buf.at[mine],
            dst_ref=buf.at[mine],
            send_sem=ssem.at[other],
            recv_sem=rsem.at[mine],
            device_id=device,
            device_id_type=MESH,
        )

    def arrival(buf, ssem, rsem, other, device):
        return pltpu.make_async_remote_copy(
            src_ref=buf.at[other],
            dst_ref=buf.at[other],
            send_sem=ssem.at[other],
            recv_sem=rsem.at[other],
            device_id=device,
            device_id_type=MESH,
        )

    for d in range(1, NY):
        other = (yc + d) % NY
        spread(vy_ref, vy_s, vy_r, yc, other, y_dev(other)).start()

    for i in range(NC - 1):
        sender = freq_peer(i)
        gram_copy(sender, sender).wait_recv()
    gx_ref[...] = total_of(gr_ref, NC)

    def gram_y(other, slot):
        return pltpu.make_async_remote_copy(
            src_ref=gx_ref.at[pl.ds(pl.multiple_of(other * gsub, gsub), gsub), :],
            dst_ref=gy_ref.at[slot],
            send_sem=gy_s.at[other],
            recv_sem=gy_r.at[slot],
            device_id=y_dev(other),
            device_id_type=MESH,
        )

    for d in range(1, NY):
        gram_y((yc + d) % NY, yc).start()
    gy_ref[yc] = gx_ref[pl.ds(pl.multiple_of(yc * gsub, gsub), gsub), :]

    for d in range(1, NY):
        other = (yc + d) % NY
        arrival(vy_ref, vy_s, vy_r, other, y_dev(other)).wait_recv()
    vz_ref[zc] = total_of(vy_ref, NY)
    for d in range(1, nz):
        other = (zc + d) % nz
        spread(vz_ref, vz_s, vz_r, zc, other, z_dev(other)).start()

    for d in range(1, NY):
        other = (yc + d) % NY
        gram_y(other, other).wait_recv()
    gz_ref[zc] = total_of(gy_ref, NY)
    for d in range(1, nz):
        other = (zc + d) % nz
        spread(gz_ref, gz_s, gz_r, zc, other, z_dev(other)).start()

    for d in range(1, nz):
        other = (zc + d) % nz
        arrival(vz_ref, vz_s, vz_r, other, z_dev(other)).wait_recv()
    v = total_of(vz_ref, nz) * (1.0 / total_rows)

    odd = (lane4 // 32) % 2 == 1
    turned = pltpu.roll(v, 64, 1)
    vr = jnp.where(lane4 < 64, v, turned)
    vi = jnp.where(lane4 < 64, turned, v)
    square = v * v
    square = square + pltpu.roll(square, 64, 1)
    norm1 = jnp.sum(jnp.where(lane4 < 32, square, 0.0), axis=1, keepdims=True) * (1.0 / NB)
    norm2 = jnp.sum(jnp.where((lane4 >= 32) & (lane4 < 64), square, 0.0), axis=1, keepdims=True)
    norm2 = norm2 * (1.0 / NB)
    scale = jnp.where(odd, 1.0 / jnp.sqrt(norm2 + 1e-06), 1.0 / jnp.sqrt(norm1 + 1e-06))
    yr = vr * scale
    yi = vi * scale
    k1re = jnp.where(odd, -pltpu.roll(yi, 32, 1), yr)
    k1im = jnp.where(odd, pltpu.roll(yr, 32, 1), yi)
    k2re = jnp.where(odd, -yi, pltpu.roll(yr, 96, 1))
    k2im = jnp.where(odd, yr, pltpu.roll(yi, 96, 1))
    pieces = []
    for p in range(per // 2):
        pieces += [w[p : p + 1] for w in (k1re, k1im, k2re, k2im)]
    e_ref[me] = jnp.concatenate(pieces, axis=0)

    def e_send(i, carry):
        to = freq_peer(i)
        spread(e_ref, e_s, e_r, me, to, {"freq": to}).start()
        return carry

    lax.fori_loop(0, NC - 1, e_send, 0)

    own = lanes((2 * per, block)) // 64 == lanes((2 * per, block), 0) // 2

    def project(owner):
        e = e_ref[owner]
        left = jnp.where(own, jnp.concatenate([e] * (block // 128), axis=1), 0.0)
        high, low = split(left)
        first = pl.multiple_of(owner * block, block)
        right = ah_ref[pl.ds(first, block), :]
        both = dot(jnp.concatenate([high, low], axis=0), right)
        out = both[: 2 * per] + both[2 * per :] + dot(high, al_ref[pl.ds(first, block), :])
        return out * inv_root

    mr_ref[me] = project(me)

    for d in range(1, nz):
        other = (zc + d) % nz
        arrival(gz_ref, gz_s, gz_r, other, z_dev(other)).wait_recv()
    gf_ref[yc] = total_of(gz_ref, nz) * (1.0 / total_rows)
    for d in range(1, NY):
        other = (yc + d) % NY
        spread(gf_ref, ga_s, ga_r, yc, other, y_dev(other)).start()

    def modes_copy(to, slot):
        return pltpu.make_async_remote_copy(
            src_ref=ms_ref.at[to],
            dst_ref=mr_ref.at[slot],
            send_sem=m_s.at[to],
            recv_sem=m_r.at[slot],
            device_id={"freq": to},
            device_id_type=MESH,
        )

    def mode_step(i, carry):
        owner = freq_peer(i)
        arrival(e_ref, e_s, e_r, owner, {"freq": owner}).wait_recv()
        ms_ref[owner] = project(owner)
        modes_copy(owner, me).start()
        return carry

    lax.fori_loop(0, NC - 1, mode_step, 0)

    for d in range(1, NY):
        other = (yc + d) % NY
        arrival(gf_ref, ga_s, ga_r, other, y_dev(other)).wait_recv()
    packed = jnp.concatenate([gf_ref[i] for i in range(NY)], axis=0)
    flipped = jnp.concatenate([packed, packed], axis=0).T
    for q in range(per // 4):
        for k in range(4):
            here = packed[q * NB : (q + 1) * NB]
            there = flipped[k * NB : (k + 1) * NB]
            here = here if k == 0 else pltpu.roll(here, 128 - 32 * k, 1)
            there = there if q == 0 else pltpu.roll(there, 128 - 32 * q, 1)
            row = (4 * q + k) * 2 * NB
            above = lanes((NB, NB), 0) <= lanes((NB, NB))
            same = lanes((NB, NB), 0) == lanes((NB, NB))
            here, there = here[:, :NB], there[:, :NB]
            gram_out[row : row + NB, :] = jnp.where(above, here, there)
            imag = jnp.where(above, -there, here)
            gram_out[row + NB : row + 2 * NB, :] = jnp.where(same, 0.0, imag)

    def modes_wait(i, carry):
        sender = freq_peer(i)
        modes_copy(sender, sender).wait_recv()
        return carry

    lax.fori_loop(0, NC - 1, modes_wait, 0)
    for s in range(NC):
        modes_out[:, s * rows : (s + 1) * rows] = mr_ref[s]

    def sent_x(i, carry):
        to = freq_peer(i)
        gram_copy(to, me).wait_send()
        vx_copy(to, me).wait_send()
        spread(e_ref, e_s, e_r, me, to, {"freq": to}).wait_send()
        modes_copy(to, me).wait_send()
        return carry

    lax.fori_loop(0, NC - 1, sent_x, 0)
    for d in range(1, NY):
        other = (yc + d) % NY
        spread(vy_ref, vy_s, vy_r, yc, other, y_dev(other)).wait_send()
        gram_y(other, yc).wait_send()
        spread(gf_ref, ga_s, ga_r, yc, other, y_dev(other)).wait_send()
    for d in range(1, nz):
        other = (zc + d) % nz
        spread(vz_ref, vz_s, vz_r, zc, other, z_dev(other)).wait_send()
        spread(gz_ref, gz_s, gz_r, zc, other, z_dev(other)).wait_send()


def shards(nz, table, snapshots, weight, start_vec):
    times, rows = snapshots.shape
    total_rows = weight.shape[0] * lax.axis_size("pts")
    per = NF // NC
    dma = pltpu.SemaphoreType.DMA
    vmem = pl.BlockSpec(memory_space=pltpu.VMEM)
    gram_rows = per // 4 * NB
    gram, modes = pl.pallas_call(
        functools.partial(kernel, nz, total_rows),
        out_shape=(
            jax.ShapeDtypeStruct((per * 2 * NB, NB), F32),
            jax.ShapeDtypeStruct((per * 2, NC * rows), F32),
        ),
        in_specs=[pl.BlockSpec(memory_space=pl.ANY), vmem, vmem, vmem],
        out_specs=(vmem, vmem),
        scratch_shapes=[
            pltpu.VMEM((times, rows), F32),
            pltpu.VMEM((times * 2, rows), BF),
            pltpu.VMEM((rows // 128, NF * 2 * PITCH, 128), F32),
            pltpu.VMEM((NF * 2 * NB, rows), BF),
            pltpu.VMEM((NF * 2 * NB, rows), BF),
            pltpu.VMEM((NC, gram_rows, 128), F32),
            pltpu.VMEM((NC, gram_rows, 128), F32),
            pltpu.VMEM((NC, per // 2, 128), F32),
            pltpu.VMEM((NC, per // 2, 128), F32),
            pltpu.VMEM((gram_rows, 128), F32),
            pltpu.VMEM((NY, gram_rows // NY, 128), F32),
            pltpu.VMEM((nz, gram_rows // NY, 128), F32),
            pltpu.VMEM((NY, gram_rows // NY, 128), F32),
            pltpu.VMEM((NY, per // 2, 128), F32),
            pltpu.VMEM((nz, per // 2, 128), F32),
            pltpu.VMEM((NC, per * 2, 128), F32),
            pltpu.VMEM((NC, per * 2, rows), F32),
            pltpu.VMEM((NC, per * 2, rows), F32),
            pltpu.VMEM((NF // 2, NB, 128), F32),
            pltpu.VMEM((NF // 2, NB, 128), F32),
            dma((8,)),
            dma((NC,)),
            dma((NC,)),
            dma((NY,)),
            dma((NY,)),
            dma((nz,)),
            dma((nz,)),
            dma((NY,)),
            dma((NY,)),
            dma((NC,)),
            dma((NC,)),
            dma((NY,)),
            dma((NY,)),
            dma((nz,)),
            dma((nz,)),
            dma((NC,)),
            dma((NC,)),
            dma((NC,)),
            dma((NC,)),
        ],
        compiler_params=pltpu.CompilerParams(collective_id=0, has_side_effects=True),
        name="spod",
    )(snapshots, weight.reshape(-1, 128), start_vec.transpose(1, 2, 0), table)
    return gram.reshape(per, 2, NB, NB), modes.reshape(per, 2, NC * rows)


def solution(mesh):
    placed = (P(None, ("pts", "freq")), P("pts"), P())
    nz = mesh.shape["pts"] // NY
    return jax.shard_map(
        functools.partial(shards, nz, dft_operand()),
        mesh=mesh,
        in_specs=placed,
        out_specs=(P("freq", None, None, None), P("freq", None, "pts")),
        check_vma=False,
    )
```

```python
import functools
import math

import jax
import jax.numpy as jnp
import numpy as np
from jax import lax
from jax.experimental import pallas as pl
from jax.experimental.pallas import tpu as pltpu
from jax.sharding import PartitionSpec as P

NFFT = 128
NB = 32
NF = 64
HALF = NFFT // 2
NC = 8
NY = 8
PITCH = NB + 1
MESH = pl.DeviceIdType.MESH
BF = jnp.bfloat16
F32 = jnp.float32


def dft_operand():
    times = np.arange(NFFT)
    phases = (np.arange(NF)[:, None] * times[None, :] % NFFT) * (2.0 * math.pi / NFFT)
    window = 0.5 - 0.5 * np.cos(times * (2.0 * math.pi / NFFT))
    window = window / np.sqrt(np.sum(window * window))
    rows = np.stack([np.cos(phases) * window, -np.sin(phases) * window], axis=1)
    rows = rows.reshape(2 * NF, NFFT).astype(np.float32)
    high = rows.astype(BF)
    low = (rows - high.astype(np.float32)).astype(BF)
    zero = np.zeros_like(low[:, :HALF])
    top = np.concatenate([high[:, :HALF], high[:, :HALF], high[:, HALF:], high[:, HALF:]], axis=1)
    bottom = np.concatenate([low[:, :HALF], zero, low[:, HALF:], zero], axis=1)
    return np.concatenate([top, bottom], axis=0)


def split(value):
    high = value.astype(BF)
    return high, (value - high.astype(F32)).astype(BF)


def dot(a, b):
    return lax.dot_general(a, b, (((1,), (0,)), ((), ())), preferred_element_type=F32)


def dot_t(a, b):
    return lax.dot_general(a, b, (((1,), (1,)), ((), ())), preferred_element_type=F32)


def lanes(shape, axis=1):
    return lax.broadcasted_iota(jnp.int32, shape, axis)


def kernel(
    nz,
    total_rows,
    snap_hbm,
    weight_ref,
    start_ref,
    table_ref,
    gram_out,
    modes_out,
    x_ref,
    xc_ref,
    q_ref,
    ah_ref,
    al_ref,
    gs_ref,
    gr_ref,
    vs_ref,
    vx_ref,
    gx_ref,
    gy_ref,
    gz_ref,
    gf_ref,
    vy_ref,
    vz_ref,
    e_ref,
    ms_ref,
    mr_ref,
    sa_ref,
    sb_ref,
    load_sem,
    gx_s,
    gx_r,
    gy_s,
    gy_r,
    gz_s,
    gz_r,
    ga_s,
    ga_r,
    vx_s,
    vx_r,
    vy_s,
    vy_r,
    vz_s,
    vz_r,
    e_s,
    e_r,
    m_s,
    m_r,
):
    halves = x_ref.shape[0] // HALF
    rows = x_ref.shape[1]
    pts = lax.axis_index("pts")
    me = lax.axis_index("freq")
    zc = pts // NY
    yc = pts % NY
    xc = me // 2
    core = me % 2

    chunks = load_sem.shape[0]
    span = x_ref.shape[0] // chunks

    def load(i):
        part = pl.ds(i * span, span)
        return pltpu.make_async_copy(snap_hbm.at[part, :], x_ref.at[part, :], load_sem.at[i])

    for i in range(chunks):
        load(i).start()

    def freq_peer(i):
        step = (2, 1, 3, 0)[i // 2]
        return ((xc + step) % (NC // 2)) * 2 + (core + 1 - i % 2) % 2

    barrier = pltpu.get_barrier_semaphore()
    for i in range(NC - 1):
        pl.semaphore_signal(barrier, inc=1, device_id={"freq": freq_peer(i)}, device_id_type=MESH)
    for d in range(1, NY):
        pl.semaphore_signal(
            barrier, inc=1, device_id={"pts": zc * NY + (yc + d) % NY}, device_id_type=MESH
        )
    for d in range(1, nz):
        pl.semaphore_signal(
            barrier, inc=1, device_id={"pts": (zc + d) % nz * NY + yc}, device_id_type=MESH
        )

    groups = rows // 128
    weight = jnp.concatenate(
        [weight_ref[pl.ds(me * groups + j, 1), :] for j in range(groups)], axis=1
    )
    root = jnp.sqrt(weight)
    inv_root = 1.0 / root
    seg = lanes((NB, 128)) // 32
    coeffs = jnp.concatenate([start_ref[0], start_ref[1]], axis=1)

    for i in range(NF // 4):
        for odd in range(2):
            r1, r2, i1, i2 = (
                jnp.broadcast_to(coeffs[:, n : n + 1], (NB, 128))
                for n in (4 * i + 2 * odd, 4 * i + 2 * odd + 1, NF + 4 * i + 2 * odd, NF + 4 * i + 2 * odd + 1)
            )
            at = seg if odd == 0 else (seg + 2) % 4
            pair = 2 * i + odd
            sa_ref[pair] = jnp.where(at == 0, r1, jnp.where(at == 1, r2, jnp.where(at == 2, i1, i2)))
            sb_ref[pair] = jnp.where(at == 0, i1, jnp.where(at == 1, i2, jnp.where(at == 2, -r1, -r2)))

    total = jnp.zeros((24, rows), F32)
    for i in range(chunks):
        load(i).wait()
        for j in range(span // 24):
            total = total + x_ref[i * span + j * 24 : i * span + (j + 1) * 24, :]
    mean = jnp.sum(total, axis=0, keepdims=True) * (1.0 / x_ref.shape[0])

    def centre(j):
        high, low = split((x_ref[j * HALF : (j + 1) * HALF, :] - mean) * root)
        xc_ref[j * NFFT : j * NFFT + HALF, :] = high
        xc_ref[j * NFFT + HALF : (j + 1) * NFFT, :] = low

    done = 0
    for b in range(0, NB, 2):
        while done < min(b + 3 + 2, halves):
            centre(done)
            done += 1
        right = jnp.concatenate(
            [xc_ref[n * NFFT : (n + 2) * NFFT, :] for n in (b, b + 1)], axis=1
        )
        both = dot(table_ref[...], right)
        value = both[: 2 * NF] + both[2 * NF :]
        for m in range(2):
            for j in range(groups):
                at = m * rows + j * 128
                q_ref[j, pl.ds(b + m, 2 * NF, stride=PITCH), :] = value[:, at : at + 128]

    pl.semaphore_wait(barrier, NC - 1 + NY - 1 + nz - 1)

    per = NF // NC
    block = per * 2 * NB

    def gram_copy(to, slot):
        return pltpu.make_async_remote_copy(
            src_ref=gs_ref.at[to],
            dst_ref=gr_ref.at[slot],
            send_sem=gx_s.at[to],
            recv_sem=gx_r.at[slot],
            device_id={"freq": to},
            device_id_type=MESH,
        )

    def vx_copy(to, slot):
        return pltpu.make_async_remote_copy(
            src_ref=vs_ref.at[to],
            dst_ref=vx_ref.at[slot],
            send_sem=vx_s.at[to],
            recv_sem=vx_r.at[slot],
            device_id={"freq": to},
            device_id_type=MESH,
        )

    upper = lanes((NB, 128), 0) <= lanes((NB, 128)) % 32
    lane4 = lanes((per // 2, 128))
    lane = lanes((NB, 128))

    def split_of(owner, p):
        first = pl.multiple_of(owner * block + p * 128, 128)
        hs, ls = [], []
        for n in range(4):
            source = (owner * (2 * per) + p * 4 + n) * PITCH
            value = [q_ref[j, pl.ds(source, NB), :] for j in range(groups)]
            high, low = split(jnp.concatenate(value, axis=1))
            ah_ref[pl.ds(first + n * NB, NB), :] = high
            al_ref[pl.ds(first + n * NB, NB), :] = low
            hs.append(high); ls.append(low)
        return hs, ls

    def operands(hs, ls, p):
        rh, ih = jnp.concatenate([hs[0], hs[2]], axis=0), jnp.concatenate([hs[1], hs[3]], axis=0)
        rl, il = jnp.concatenate([ls[0], ls[2]], axis=0), jnp.concatenate([ls[1], ls[3]], axis=0)
        h1 = jnp.concatenate([rh, ih], axis=1)
        l1 = jnp.concatenate([rl, il], axis=1)
        h2 = jnp.concatenate([ih, -rh], axis=1)
        l2 = jnp.concatenate([il, -rl], axis=1)
        right = [h1, h2, l1, l2] if p % 2 == 0 else [h2, h1, l2, l1]
        return jnp.concatenate([h1, l1], axis=0), jnp.concatenate(right, axis=0)

    def gram_of(owner):
        parts_a, parts_b, packed = [], [], None
        for p in range(per // 2):
            left, right = operands(*split_of(owner, p), p)
            out = dot_t(left, right)
            z = out[0:64, 0:128] + (out[0:64, 128:256] + out[64:128, 0:128])
            g = jnp.where(seg % 2 == 0, z[0:32], z[32:64])
            pair = owner * (per // 2) + p
            parts_a.append(jnp.sum(g * sa_ref[pair], axis=0, keepdims=True))
            parts_b.append(jnp.sum(g * sb_ref[pair], axis=0, keepdims=True))
            half = jnp.where(upper, g, pltpu.roll(g, 64, 1))
            if p % 2 == 0:
                packed = half
            else:
                both = jnp.where(lane < 64, packed, half)
                gs_ref[owner, pl.ds(p // 2 * NB, NB), :] = both
        va = jnp.concatenate(parts_a, axis=0)
        vb = jnp.concatenate(parts_b, axis=0)
        vs_ref[owner] = jnp.where(
            lane4 < 64, va + pltpu.roll(va, 64, 1), vb + pltpu.roll(vb, 64, 1)
        )

    def gram_step(i):
        owner = freq_peer(i)
        gram_of(owner)
        vx_copy(owner, me).start()
        gram_copy(owner, me).start()

    for i in range(NC - 1):
        gram_step(i)
    gram_of(me)
    vx_ref[me] = vs_ref[me]
    gr_ref[me] = gs_ref[me]

    def total_of(buf, n):
        out = buf[0]
        for i in range(1, n):
            out = out + buf[i]
        return out

    for i in range(NC - 1):
        sender = freq_peer(i)
        vx_copy(sender, sender).wait_recv()
    vy_ref[yc] = total_of(vx_ref, NC)

    gsub = gx_ref.shape[0] // NY

    def y_dev(other):
        return {"pts": zc * NY + other}

    def z_dev(other):
        return {"pts": other * NY + yc}

    def spread(buf, ssem, rsem, mine, other, device):
        return pltpu.make_async_remote_copy(
            src_ref=buf.at[mine],
            dst_ref=buf.at[mine],
            send_sem=ssem.at[other],
            recv_sem=rsem.at[mine],
            device_id=device,
            device_id_type=MESH,
        )

    def arrival(buf, ssem, rsem, other, device):
        return pltpu.make_async_remote_copy(
            src_ref=buf.at[other],
            dst_ref=buf.at[other],
            send_sem=ssem.at[other],
            recv_sem=rsem.at[other],
            device_id=device,
            device_id_type=MESH,
        )

    for d in range(1, NY):
        other = (yc + d) % NY
        spread(vy_ref, vy_s, vy_r, yc, other, y_dev(other)).start()

    for i in range(NC - 1):
        sender = freq_peer(i)
        gram_copy(sender, sender).wait_recv()
    gx_ref[...] = total_of(gr_ref, NC)

    def gram_y(other, slot):
        return pltpu.make_async_remote_copy(
            src_ref=gx_ref.at[pl.ds(pl.multiple_of(other * gsub, gsub), gsub), :],
            dst_ref=gy_ref.at[slot],
            send_sem=gy_s.at[other],
            recv_sem=gy_r.at[slot],
            device_id=y_dev(other),
            device_id_type=MESH,
        )

    for d in range(1, NY):
        gram_y((yc + d) % NY, yc).start()
    gy_ref[yc] = gx_ref[pl.ds(pl.multiple_of(yc * gsub, gsub), gsub), :]

    for d in range(1, NY):
        other = (yc + d) % NY
        arrival(vy_ref, vy_s, vy_r, other, y_dev(other)).wait_recv()
    vz_ref[zc] = total_of(vy_ref, NY)
    for d in range(1, nz):
        other = (zc + d) % nz
        spread(vz_ref, vz_s, vz_r, zc, other, z_dev(other)).start()

    for d in range(1, NY):
        other = (yc + d) % NY
        gram_y(other, other).wait_recv()
    gz_ref[zc] = total_of(gy_ref, NY)
    for d in range(1, nz):
        other = (zc + d) % nz
        spread(gz_ref, gz_s, gz_r, zc, other, z_dev(other)).start()

    for d in range(1, nz):
        other = (zc + d) % nz
        arrival(vz_ref, vz_s, vz_r, other, z_dev(other)).wait_recv()
    v = total_of(vz_ref, nz) * (1.0 / total_rows)

    odd = (lane4 // 32) % 2 == 1
    turned = pltpu.roll(v, 64, 1)
    vr = jnp.where(lane4 < 64, v, turned)
    vi = jnp.where(lane4 < 64, turned, v)
    square = v * v
    square = square + pltpu.roll(square, 64, 1)
    norm1 = jnp.sum(jnp.where(lane4 < 32, square, 0.0), axis=1, keepdims=True) * (1.0 / NB)
    norm2 = jnp.sum(jnp.where((lane4 >= 32) & (lane4 < 64), square, 0.0), axis=1, keepdims=True)
    norm2 = norm2 * (1.0 / NB)
    scale = jnp.where(odd, 1.0 / jnp.sqrt(norm2 + 1e-06), 1.0 / jnp.sqrt(norm1 + 1e-06))
    yr = vr * scale
    yi = vi * scale
    k1re = jnp.where(odd, -pltpu.roll(yi, 32, 1), yr)
    k1im = jnp.where(odd, pltpu.roll(yr, 32, 1), yi)
    k2re = jnp.where(odd, -yi, pltpu.roll(yr, 96, 1))
    k2im = jnp.where(odd, yr, pltpu.roll(yi, 96, 1))
    pieces = []
    for p in range(per // 2):
        pieces += [w[p : p + 1] for w in (k1re, k1im, k2re, k2im)]
    e_ref[me] = jnp.concatenate(pieces, axis=0)

    for i in range(NC - 1):
        to = freq_peer(i)
        spread(e_ref, e_s, e_r, me, to, {"freq": to}).start()

    own = lanes((2 * per, block)) // 64 == lanes((2 * per, block), 0) // 2

    def project(owner):
        e = e_ref[owner]
        left = jnp.where(own, jnp.concatenate([e] * (block // 128), axis=1), 0.0)
        high, low = split(left)
        first = pl.multiple_of(owner * block, block)
        right = ah_ref[pl.ds(first, block), :]
        both = dot(jnp.concatenate([high, low], axis=0), right)
        out = both[: 2 * per] + both[2 * per :] + dot(high, al_ref[pl.ds(first, block), :])
        return out * inv_root

    mr_ref[me] = project(me)

    for d in range(1, nz):
        other = (zc + d) % nz
        arrival(gz_ref, gz_s, gz_r, other, z_dev(other)).wait_recv()
    gf_ref[yc] = total_of(gz_ref, nz) * (1.0 / total_rows)
    for d in range(1, NY):
        other = (yc + d) % NY
        spread(gf_ref, ga_s, ga_r, yc, other, y_dev(other)).start()

    def modes_copy(to, slot):
        return pltpu.make_async_remote_copy(
            src_ref=ms_ref.at[to],
            dst_ref=mr_ref.at[slot],
            send_sem=m_s.at[to],
            recv_sem=m_r.at[slot],
            device_id={"freq": to},
            device_id_type=MESH,
        )

    for step in ((6,), (2, 3), (4, 5), (0, 1)):
        owners = [freq_peer(i) for i in step]
        for owner in owners:
            arrival(e_ref, e_s, e_r, owner, {"freq": owner}).wait_recv()
        values = [project(owner) for owner in owners]
        for owner, value in zip(owners, values):
            ms_ref[owner] = value
        for owner in owners:
            modes_copy(owner, me).start()

    for d in range(1, NY):
        other = (yc + d) % NY
        arrival(gf_ref, ga_s, ga_r, other, y_dev(other)).wait_recv()
    packed = jnp.concatenate([gf_ref[i] for i in range(NY)], axis=0)
    flipped = jnp.concatenate([packed, packed], axis=0).T
    for q in range(per // 4):
        for k in range(4):
            here = packed[q * NB : (q + 1) * NB]
            there = flipped[k * NB : (k + 1) * NB]
            here = here if k == 0 else pltpu.roll(here, 128 - 32 * k, 1)
            there = there if q == 0 else pltpu.roll(there, 128 - 32 * q, 1)
            row = (4 * q + k) * 2 * NB
            above = lanes((NB, NB), 0) <= lanes((NB, NB))
            same = lanes((NB, NB), 0) == lanes((NB, NB))
            here, there = here[:, :NB], there[:, :NB]
            gram_out[row : row + NB, :] = jnp.where(above, here, there)
            imag = jnp.where(above, -there, here)
            gram_out[row + NB : row + 2 * NB, :] = jnp.where(same, 0.0, imag)

    for i in range(NC - 1):
        to = freq_peer(i)
        gram_copy(to, me).wait_send()
        vx_copy(to, me).wait_send()
        spread(e_ref, e_s, e_r, me, to, {"freq": to}).wait_send()
    for d in range(1, NY):
        other = (yc + d) % NY
        spread(vy_ref, vy_s, vy_r, yc, other, y_dev(other)).wait_send()
        gram_y(other, yc).wait_send()
        spread(gf_ref, ga_s, ga_r, yc, other, y_dev(other)).wait_send()
    for d in range(1, nz):
        other = (zc + d) % nz
        spread(vz_ref, vz_s, vz_r, zc, other, z_dev(other)).wait_send()
        spread(gz_ref, gz_s, gz_r, zc, other, z_dev(other)).wait_send()

    for i in (6, 2, 3, 4, 5, 0, 1):
        sender = freq_peer(i)
        modes_copy(sender, sender).wait_recv()
    for s in range(NC):
        modes_out[:, s * rows : (s + 1) * rows] = mr_ref[s]
    for i in range(NC - 1):
        modes_copy(freq_peer(i), me).wait_send()


def shards(nz, table, snapshots, weight, start_vec):
    times, rows = snapshots.shape
    total_rows = weight.shape[0] * lax.axis_size("pts")
    per = NF // NC
    dma = pltpu.SemaphoreType.DMA
    vmem = pl.BlockSpec(memory_space=pltpu.VMEM)
    gram_rows = per // 4 * NB
    gram, modes = pl.pallas_call(
        functools.partial(kernel, nz, total_rows),
        out_shape=(
            jax.ShapeDtypeStruct((per * 2 * NB, NB), F32),
            jax.ShapeDtypeStruct((per * 2, NC * rows), F32),
        ),
        in_specs=[pl.BlockSpec(memory_space=pl.ANY), vmem, vmem, vmem],
        out_specs=(vmem, vmem),
        scratch_shapes=[
            pltpu.VMEM((times, rows), F32),
            pltpu.VMEM((times * 2, rows), BF),
            pltpu.VMEM((rows // 128, NF * 2 * PITCH, 128), F32),
            pltpu.VMEM((NF * 2 * NB, rows), BF),
            pltpu.VMEM((NF * 2 * NB, rows), BF),
            pltpu.VMEM((NC, gram_rows, 128), F32),
            pltpu.VMEM((NC, gram_rows, 128), F32),
            pltpu.VMEM((NC, per // 2, 128), F32),
            pltpu.VMEM((NC, per // 2, 128), F32),
            pltpu.VMEM((gram_rows, 128), F32),
            pltpu.VMEM((NY, gram_rows // NY, 128), F32),
            pltpu.VMEM((nz, gram_rows // NY, 128), F32),
            pltpu.VMEM((NY, gram_rows // NY, 128), F32),
            pltpu.VMEM((NY, per // 2, 128), F32),
            pltpu.VMEM((nz, per // 2, 128), F32),
            pltpu.VMEM((NC, per * 2, 128), F32),
            pltpu.VMEM((NC, per * 2, rows), F32),
            pltpu.VMEM((NC, per * 2, rows), F32),
            pltpu.VMEM((NF // 2, NB, 128), F32),
            pltpu.VMEM((NF // 2, NB, 128), F32),
            dma((8,)),
            dma((NC,)),
            dma((NC,)),
            dma((NY,)),
            dma((NY,)),
            dma((nz,)),
            dma((nz,)),
            dma((NY,)),
            dma((NY,)),
            dma((NC,)),
            dma((NC,)),
            dma((NY,)),
            dma((NY,)),
            dma((nz,)),
            dma((nz,)),
            dma((NC,)),
            dma((NC,)),
            dma((NC,)),
            dma((NC,)),
        ],
        compiler_params=pltpu.CompilerParams(collective_id=0, has_side_effects=True),
        name="spod",
    )(snapshots, weight.reshape(-1, 128), start_vec.transpose(1, 2, 0), table)
    return gram.reshape(per, 2, NB, NB), modes.reshape(per, 2, NC * rows)


def solution(mesh):
    placed = (P(None, ("pts", "freq")), P("pts"), P())
    nz = mesh.shape["pts"] // NY
    return jax.shard_map(
        functools.partial(shards, nz, dft_operand()),
        mesh=mesh,
        in_specs=placed,
        out_specs=(P("freq", None, None, None), P("freq", None, "pts")),
        check_vma=False,
    )
```

```python
import functools
import math

import jax
import jax.numpy as jnp
import numpy as np
from jax import lax
from jax.experimental import pallas as pl
from jax.experimental.pallas import tpu as pltpu
from jax.sharding import PartitionSpec as P

NFFT = 128
NB = 32
NF = 64
HALF = NFFT // 2
NC = 8
NY = 8
PITCH = NB + 1
MESH = pl.DeviceIdType.MESH
BF = jnp.bfloat16
F32 = jnp.float32


def dft_operand():
    times = np.arange(NFFT)
    phases = (np.arange(NF)[:, None] * times[None, :] % NFFT) * (2.0 * math.pi / NFFT)
    window = 0.5 - 0.5 * np.cos(times * (2.0 * math.pi / NFFT))
    window = window / np.sqrt(np.sum(window * window))
    rows = np.stack([np.cos(phases) * window, -np.sin(phases) * window], axis=1)
    rows = rows.reshape(2 * NF, NFFT).astype(np.float32)
    high = rows.astype(BF)
    low = (rows - high.astype(np.float32)).astype(BF)
    zero = np.zeros_like(low[:, :HALF])
    top = np.concatenate([high[:, :HALF], high[:, :HALF], high[:, HALF:], high[:, HALF:]], axis=1)
    bottom = np.concatenate([low[:, :HALF], zero, low[:, HALF:], zero], axis=1)
    return np.concatenate([top, bottom], axis=0)


def split(value):
    high = value.astype(BF)
    return high, (value - high.astype(F32)).astype(BF)


def dot(a, b):
    return lax.dot_general(a, b, (((1,), (0,)), ((), ())), preferred_element_type=F32)


def dot_t(a, b):
    return lax.dot_general(a, b, (((1,), (1,)), ((), ())), preferred_element_type=F32)


def lanes(shape, axis=1):
    return lax.broadcasted_iota(jnp.int32, shape, axis)


def kernel(
    nz,
    total_rows,
    snap_hbm,
    weight_hbm,
    start_hbm,
    table_hbm,
    gram_out,
    modes_out,
    weight_ref,
    start_ref,
    table_ref,
    x_ref,
    xc_ref,
    q_ref,
    ah_ref,
    al_ref,
    gs_ref,
    gr_ref,
    vs_ref,
    vx_ref,
    gx_ref,
    gy_ref,
    gz_ref,
    gf_ref,
    vy_ref,
    vz_ref,
    e_ref,
    ms_ref,
    mr_ref,
    sa_ref,
    sb_ref,
    small_sem,
    load_sem,
    gx_s,
    gx_r,
    gy_s,
    gy_r,
    gz_s,
    gz_r,
    ga_s,
    ga_r,
    vx_s,
    vx_r,
    vy_s,
    vy_r,
    vz_s,
    vz_r,
    e_s,
    e_r,
    m_s,
    m_r,
):
    halves = x_ref.shape[0] // HALF
    rows = x_ref.shape[1]
    pts = lax.axis_index("pts")
    me = lax.axis_index("freq")
    zc = pts // NY
    yc = pts % NY
    xc = me // 2
    core = me % 2

    chunks = load_sem.shape[0]
    span = x_ref.shape[0] // chunks

    def load(i):
        part = pl.ds(i * span, span)
        return pltpu.make_async_copy(snap_hbm.at[part, :], x_ref.at[part, :], load_sem.at[i])

    small = [
        pltpu.make_async_copy(source, target, small_sem.at[i])
        for i, (source, target) in enumerate(
            ((start_hbm, start_ref), (weight_hbm, weight_ref), (table_hbm, table_ref))
        )
    ]
    for copy in small[:2]:
        copy.start()
    for i in range(chunks):
        load(i).start()
    small[2].start()

    def freq_peer(i):
        step = (2, 1, 3, 0)[i // 2]
        return ((xc + step) % (NC // 2)) * 2 + (core + 1 - i % 2) % 2

    barrier = pltpu.get_barrier_semaphore()
    for i in range(NC - 1):
        pl.semaphore_signal(barrier, inc=1, device_id={"freq": freq_peer(i)}, device_id_type=MESH)
    for d in range(1, NY):
        pl.semaphore_signal(
            barrier, inc=1, device_id={"pts": zc * NY + (yc + d) % NY}, device_id_type=MESH
        )
    for d in range(1, nz):
        pl.semaphore_signal(
            barrier, inc=1, device_id={"pts": (zc + d) % nz * NY + yc}, device_id_type=MESH
        )

    small[0].wait()
    small[1].wait()

    groups = rows // 128
    weight = jnp.concatenate(
        [weight_ref[pl.ds(me * groups + j, 1), :] for j in range(groups)], axis=1
    )
    root = jnp.sqrt(weight)
    inv_root = 1.0 / root
    seg = lanes((NB, 128)) // 32
    coeffs = jnp.concatenate([start_ref[0], start_ref[1]], axis=1)

    for i in range(NF // 4):
        for odd in range(2):
            r1, r2, i1, i2 = (
                jnp.broadcast_to(coeffs[:, n : n + 1], (NB, 128))
                for n in (4 * i + 2 * odd, 4 * i + 2 * odd + 1, NF + 4 * i + 2 * odd, NF + 4 * i + 2 * odd + 1)
            )
            at = seg if odd == 0 else (seg + 2) % 4
            pair = 2 * i + odd
            sa_ref[pair] = jnp.where(at == 0, r1, jnp.where(at == 1, r2, jnp.where(at == 2, i1, i2)))
            sb_ref[pair] = jnp.where(at == 0, i1, jnp.where(at == 1, i2, jnp.where(at == 2, -r1, -r2)))

    total = jnp.zeros((24, rows), F32)
    for i in range(chunks):
        load(i).wait()
        for j in range(span // 24):
            total = total + x_ref[i * span + j * 24 : i * span + (j + 1) * 24, :]
    mean = jnp.sum(total, axis=0, keepdims=True) * (1.0 / x_ref.shape[0])

    small[2].wait()

    def centre(j):
        high, low = split((x_ref[j * HALF : (j + 1) * HALF, :] - mean) * root)
        xc_ref[j * NFFT : j * NFFT + HALF, :] = high
        xc_ref[j * NFFT + HALF : (j + 1) * NFFT, :] = low

    done = 0
    for b in range(0, NB, 2):
        while done < min(b + 3 + 2, halves):
            centre(done)
            done += 1
        right = jnp.concatenate(
            [xc_ref[n * NFFT : (n + 2) * NFFT, :] for n in (b, b + 1)], axis=1
        )
        both = dot(table_ref[...], right)
        value = both[: 2 * NF] + both[2 * NF :]
        for m in range(2):
            for j in range(groups):
                at = m * rows + j * 128
                q_ref[j, pl.ds(b + m, 2 * NF, stride=PITCH), :] = value[:, at : at + 128]

    pl.semaphore_wait(barrier, NC - 1 + NY - 1 + nz - 1)

    per = NF // NC
    block = per * 2 * NB

    def gram_copy(to, slot):
        return pltpu.make_async_remote_copy(
            src_ref=gs_ref.at[to],
            dst_ref=gr_ref.at[slot],
            send_sem=gx_s.at[to],
            recv_sem=gx_r.at[slot],
            device_id={"freq": to},
            device_id_type=MESH,
        )

    def vx_copy(to, slot):
        return pltpu.make_async_remote_copy(
            src_ref=vs_ref.at[to],
            dst_ref=vx_ref.at[slot],
            send_sem=vx_s.at[to],
            recv_sem=vx_r.at[slot],
            device_id={"freq": to},
            device_id_type=MESH,
        )

    upper = lanes((NB, 128), 0) <= lanes((NB, 128)) % 32
    lane4 = lanes((per // 2, 128))
    lane = lanes((NB, 128))

    def split_of(owner, p):
        first = pl.multiple_of(owner * block + p * 128, 128)
        hs, ls = [], []
        for n in range(4):
            source = (owner * (2 * per) + p * 4 + n) * PITCH
            value = [q_ref[j, pl.ds(source, NB), :] for j in range(groups)]
            high, low = split(jnp.concatenate(value, axis=1))
            ah_ref[pl.ds(first + n * NB, NB), :] = high
            al_ref[pl.ds(first + n * NB, NB), :] = low
            hs.append(high); ls.append(low)
        return hs, ls

    def operands(hs, ls, p):
        rh, ih = jnp.concatenate([hs[0], hs[2]], axis=0), jnp.concatenate([hs[1], hs[3]], axis=0)
        rl, il = jnp.concatenate([ls[0], ls[2]], axis=0), jnp.concatenate([ls[1], ls[3]], axis=0)
        h1 = jnp.concatenate([rh, ih], axis=1)
        l1 = jnp.concatenate([rl, il], axis=1)
        h2 = jnp.concatenate([ih, -rh], axis=1)
        l2 = jnp.concatenate([il, -rl], axis=1)
        right = [h1, h2, l1, l2] if p % 2 == 0 else [h2, h1, l2, l1]
        return jnp.concatenate([h1, l1], axis=0), jnp.concatenate(right, axis=0)

    def gram_of(owner):
        parts_a, parts_b, packed = [], [], None
        for p in range(per // 2):
            left, right = operands(*split_of(owner, p), p)
            out = dot_t(left, right)
            z = out[0:64, 0:128] + (out[0:64, 128:256] + out[64:128, 0:128])
            g = jnp.where(seg % 2 == 0, z[0:32], z[32:64])
            pair = owner * (per // 2) + p
            parts_a.append(jnp.sum(g * sa_ref[pair], axis=0, keepdims=True))
            parts_b.append(jnp.sum(g * sb_ref[pair], axis=0, keepdims=True))
            half = jnp.where(upper, g, pltpu.roll(g, 64, 1))
            if p % 2 == 0:
                packed = half
            else:
                both = jnp.where(lane < 64, packed, half)
                gs_ref[owner, pl.ds(p // 2 * NB, NB), :] = both
        va = jnp.concatenate(parts_a, axis=0)
        vb = jnp.concatenate(parts_b, axis=0)
        vs_ref[owner] = jnp.where(
            lane4 < 64, va + pltpu.roll(va, 64, 1), vb + pltpu.roll(vb, 64, 1)
        )

    def gram_step(i):
        owner = freq_peer(i)
        gram_of(owner)
        vx_copy(owner, me).start()
        gram_copy(owner, me).start()

    for i in range(NC - 1):
        gram_step(i)
    gram_of(me)
    vx_ref[me] = vs_ref[me]
    gr_ref[me] = gs_ref[me]

    def total_of(buf, n):
        out = buf[0]
        for i in range(1, n):
            out = out + buf[i]
        return out

    for i in range(NC - 1):
        sender = freq_peer(i)
        vx_copy(sender, sender).wait_recv()
    vy_ref[yc] = total_of(vx_ref, NC)

    gsub = gx_ref.shape[0] // NY

    def y_dev(other):
        return {"pts": zc * NY + other}

    def z_dev(other):
        return {"pts": other * NY + yc}

    def spread(buf, ssem, rsem, mine, other, device):
        return pltpu.make_async_remote_copy(
            src_ref=buf.at[mine],
            dst_ref=buf.at[mine],
            send_sem=ssem.at[other],
            recv_sem=rsem.at[mine],
            device_id=device,
            device_id_type=MESH,
        )

    def arrival(buf, ssem, rsem, other, device):
        return pltpu.make_async_remote_copy(
            src_ref=buf.at[other],
            dst_ref=buf.at[other],
            send_sem=ssem.at[other],
            recv_sem=rsem.at[other],
            device_id=device,
            device_id_type=MESH,
        )

    for d in range(1, NY):
        other = (yc + d) % NY
        spread(vy_ref, vy_s, vy_r, yc, other, y_dev(other)).start()

    for i in range(NC - 1):
        sender = freq_peer(i)
        gram_copy(sender, sender).wait_recv()
    gx_ref[...] = total_of(gr_ref, NC)

    def gram_y(other, slot):
        return pltpu.make_async_remote_copy(
            src_ref=gx_ref.at[pl.ds(pl.multiple_of(other * gsub, gsub), gsub), :],
            dst_ref=gy_ref.at[slot],
            send_sem=gy_s.at[other],
            recv_sem=gy_r.at[slot],
            device_id=y_dev(other),
            device_id_type=MESH,
        )

    for d in range(1, NY):
        gram_y((yc + d) % NY, yc).start()
    gy_ref[yc] = gx_ref[pl.ds(pl.multiple_of(yc * gsub, gsub), gsub), :]

    for d in range(1, NY):
        other = (yc + d) % NY
        arrival(vy_ref, vy_s, vy_r, other, y_dev(other)).wait_recv()
    vz_ref[zc] = total_of(vy_ref, NY)
    for d in range(1, nz):
        other = (zc + d) % nz
        spread(vz_ref, vz_s, vz_r, zc, other, z_dev(other)).start()

    for d in range(1, NY):
        other = (yc + d) % NY
        gram_y(other, other).wait_recv()
    gz_ref[zc] = total_of(gy_ref, NY)
    for d in range(1, nz):
        other = (zc + d) % nz
        spread(gz_ref, gz_s, gz_r, zc, other, z_dev(other)).start()

    for d in range(1, nz):
        other = (zc + d) % nz
        arrival(vz_ref, vz_s, vz_r, other, z_dev(other)).wait_recv()
    v = total_of(vz_ref, nz) * (1.0 / total_rows)

    odd = (lane4 // 32) % 2 == 1
    turned = pltpu.roll(v, 64, 1)
    vr = jnp.where(lane4 < 64, v, turned)
    vi = jnp.where(lane4 < 64, turned, v)
    square = v * v
    square = square + pltpu.roll(square, 64, 1)
    norm1 = jnp.sum(jnp.where(lane4 < 32, square, 0.0), axis=1, keepdims=True) * (1.0 / NB)
    norm2 = jnp.sum(jnp.where((lane4 >= 32) & (lane4 < 64), square, 0.0), axis=1, keepdims=True)
    norm2 = norm2 * (1.0 / NB)
    scale = jnp.where(odd, 1.0 / jnp.sqrt(norm2 + 1e-06), 1.0 / jnp.sqrt(norm1 + 1e-06))
    yr = vr * scale
    yi = vi * scale
    k1re = jnp.where(odd, -pltpu.roll(yi, 32, 1), yr)
    k1im = jnp.where(odd, pltpu.roll(yr, 32, 1), yi)
    k2re = jnp.where(odd, -yi, pltpu.roll(yr, 96, 1))
    k2im = jnp.where(odd, yr, pltpu.roll(yi, 96, 1))
    pieces = []
    for p in range(per // 2):
        pieces += [w[p : p + 1] for w in (k1re, k1im, k2re, k2im)]
    e_ref[me] = jnp.concatenate(pieces, axis=0)

    for i in range(NC - 1):
        to = freq_peer(i)
        spread(e_ref, e_s, e_r, me, to, {"freq": to}).start()

    own = lanes((2 * per, block)) // 64 == lanes((2 * per, block), 0) // 2

    def project(owner):
        e = e_ref[owner]
        left = jnp.where(own, jnp.concatenate([e] * (block // 128), axis=1), 0.0)
        high, low = split(left)
        first = pl.multiple_of(owner * block, block)
        right = ah_ref[pl.ds(first, block), :]
        both = dot(jnp.concatenate([high, low], axis=0), right)
        out = both[: 2 * per] + both[2 * per :] + dot(high, al_ref[pl.ds(first, block), :])
        return out * inv_root

    mr_ref[me] = project(me)

    for d in range(1, nz):
        other = (zc + d) % nz
        arrival(gz_ref, gz_s, gz_r, other, z_dev(other)).wait_recv()
    gf_ref[yc] = total_of(gz_ref, nz) * (1.0 / total_rows)
    for d in range(1, NY):
        other = (yc + d) % NY
        spread(gf_ref, ga_s, ga_r, yc, other, y_dev(other)).start()

    def modes_copy(to, slot):
        return pltpu.make_async_remote_copy(
            src_ref=ms_ref.at[to],
            dst_ref=mr_ref.at[slot],
            send_sem=m_s.at[to],
            recv_sem=m_r.at[slot],
            device_id={"freq": to},
            device_id_type=MESH,
        )

    for step in ((6,), (2, 3), (4, 5), (0, 1)):
        owners = [freq_peer(i) for i in step]
        for owner in owners:
            arrival(e_ref, e_s, e_r, owner, {"freq": owner}).wait_recv()
        values = [project(owner) for owner in owners]
        for owner, value in zip(owners, values):
            ms_ref[owner] = value
        for owner in owners:
            modes_copy(owner, me).start()

    for d in range(1, NY):
        other = (yc + d) % NY
        arrival(gf_ref, ga_s, ga_r, other, y_dev(other)).wait_recv()
    for i in range(NY):
        gram_out[i * gsub : (i + 1) * gsub, :] = gf_ref[i]

    for i in range(NC - 1):
        to = freq_peer(i)
        gram_copy(to, me).wait_send()
        vx_copy(to, me).wait_send()
        spread(e_ref, e_s, e_r, me, to, {"freq": to}).wait_send()
    for d in range(1, NY):
        other = (yc + d) % NY
        spread(vy_ref, vy_s, vy_r, yc, other, y_dev(other)).wait_send()
        gram_y(other, yc).wait_send()
        spread(gf_ref, ga_s, ga_r, yc, other, y_dev(other)).wait_send()
    for d in range(1, nz):
        other = (zc + d) % nz
        spread(vz_ref, vz_s, vz_r, zc, other, z_dev(other)).wait_send()
        spread(gz_ref, gz_s, gz_r, zc, other, z_dev(other)).wait_send()

    for i in (6, 2, 3, 4, 5, 0, 1):
        sender = freq_peer(i)
        modes_copy(sender, sender).wait_recv()
    for s in range(NC):
        modes_out[s] = mr_ref[s]
    for i in range(NC - 1):
        modes_copy(freq_peer(i), me).wait_send()


def finish(gram_ref, modes_ref, gram_out, modes_out):
    rows = modes_ref.shape[2]
    per = modes_ref.shape[1] // 2
    for s in range(NC):
        value = modes_ref[s]
        for k in range(per):
            modes_out[k, :, s * rows : (s + 1) * rows] = value[2 * k : 2 * k + 2]
    packed = gram_ref[...]
    flipped = jnp.concatenate([packed, packed], axis=0).T
    above = lanes((NB, NB), 0) <= lanes((NB, NB))
    same = lanes((NB, NB), 0) == lanes((NB, NB))
    for q in range(per // 4):
        for k in range(4):
            here = packed[q * NB : (q + 1) * NB]
            there = flipped[k * NB : (k + 1) * NB]
            here = here if k == 0 else pltpu.roll(here, 128 - 32 * k, 1)
            there = there if q == 0 else pltpu.roll(there, 128 - 32 * q, 1)
            here, there = here[:, :NB], there[:, :NB]
            gram_out[4 * q + k, 0] = jnp.where(above, here, there)
            gram_out[4 * q + k, 1] = jnp.where(same, 0.0, jnp.where(above, -there, here))


def shards(nz, table, snapshots, weight, start_vec):
    times, rows = snapshots.shape
    total_rows = weight.shape[0] * lax.axis_size("pts")
    per = NF // NC
    dma = pltpu.SemaphoreType.DMA
    vmem = pl.BlockSpec(memory_space=pltpu.VMEM)
    gram_rows = per // 4 * NB
    gram, modes = pl.pallas_call(
        functools.partial(kernel, nz, total_rows),
        out_shape=(
            jax.ShapeDtypeStruct((gram_rows, 128), F32),
            jax.ShapeDtypeStruct((NC, per * 2, rows), F32),
        ),
        in_specs=[pl.BlockSpec(memory_space=pltpu.HBM)] * 4,
        out_specs=(vmem, vmem),
        scratch_shapes=[
            pltpu.VMEM((weight.shape[0] // 128, 128), F32),
            pltpu.VMEM((2, NB, NF), F32),
            pltpu.VMEM(table.shape, BF),
            pltpu.VMEM((times, rows), F32),
            pltpu.VMEM((times * 2, rows), BF),
            pltpu.VMEM((rows // 128, NF * 2 * PITCH, 128), F32),
            pltpu.VMEM((NF * 2 * NB, rows), BF),
            pltpu.VMEM((NF * 2 * NB, rows), BF),
            pltpu.VMEM((NC, gram_rows, 128), F32),
            pltpu.VMEM((NC, gram_rows, 128), F32),
            pltpu.VMEM((NC, per // 2, 128), F32),
            pltpu.VMEM((NC, per // 2, 128), F32),
            pltpu.VMEM((gram_rows, 128), F32),
            pltpu.VMEM((NY, gram_rows // NY, 128), F32),
            pltpu.VMEM((nz, gram_rows // NY, 128), F32),
            pltpu.VMEM((NY, gram_rows // NY, 128), F32),
            pltpu.VMEM((NY, per // 2, 128), F32),
            pltpu.VMEM((nz, per // 2, 128), F32),
            pltpu.VMEM((NC, per * 2, 128), F32),
            pltpu.VMEM((NC, per * 2, rows), F32),
            pltpu.VMEM((NC, per * 2, rows), F32),
            pltpu.VMEM((NF // 2, NB, 128), F32),
            pltpu.VMEM((NF // 2, NB, 128), F32),
            dma((3,)),
            dma((8,)),
            dma((NC,)),
            dma((NC,)),
            dma((NY,)),
            dma((NY,)),
            dma((nz,)),
            dma((nz,)),
            dma((NY,)),
            dma((NY,)),
            dma((NC,)),
            dma((NC,)),
            dma((NY,)),
            dma((NY,)),
            dma((nz,)),
            dma((nz,)),
            dma((NC,)),
            dma((NC,)),
            dma((NC,)),
            dma((NC,)),
        ],
        compiler_params=pltpu.CompilerParams(
            collective_id=0, has_side_effects=True, vmem_limit_bytes=40 * 1024 * 1024
        ),
        name="spod",
    )(
        *(
            pltpu.with_memory_space_constraint(a, pltpu.HBM)
            for a in (snapshots, weight.reshape(-1, 128), start_vec.transpose(1, 2, 0), jnp.asarray(table))
        )
    )
    return pl.pallas_call(
        finish,
        out_shape=(
            jax.ShapeDtypeStruct((per, 2, NB, NB), F32),
            jax.ShapeDtypeStruct((per, 2, NC * rows), F32),
        ),
        in_specs=[vmem, vmem],
        out_specs=(vmem, vmem),
        compiler_params=pltpu.CompilerParams(vmem_limit_bytes=16 * 1024 * 1024),
        name="finish",
    )(gram, modes)


def solution(mesh):
    placed = (P(None, ("pts", "freq")), P("pts"), P())
    nz = mesh.shape["pts"] // NY
    return jax.shard_map(
        functools.partial(shards, nz, dft_operand()),
        mesh=mesh,
        in_specs=placed,
        out_specs=(P("freq", None, None, None), P("freq", None, "pts")),
        check_vma=False,
    )
```

```python
import functools
import math

import jax
import jax.numpy as jnp
import numpy as np
from jax import lax
from jax.experimental import pallas as pl
from jax.experimental.pallas import tpu as pltpu
from jax.sharding import PartitionSpec as P

NFFT = 128
NB = 32
NF = 64
HALF = NFFT // 2
NC = 8
NY = 8
PITCH = NB + 1
MESH = pl.DeviceIdType.MESH
BF = jnp.bfloat16
F32 = jnp.float32


def dft_operand():
    times = np.arange(NFFT)
    phases = (np.arange(NF)[:, None] * times[None, :] % NFFT) * (2.0 * math.pi / NFFT)
    window = 0.5 - 0.5 * np.cos(times * (2.0 * math.pi / NFFT))
    window = window / np.sqrt(np.sum(window * window))
    rows = np.stack([np.cos(phases) * window, -np.sin(phases) * window], axis=1)
    rows = rows.reshape(2 * NF, NFFT).astype(np.float32)
    high = rows.astype(BF)
    low = (rows - high.astype(np.float32)).astype(BF)
    zero = np.zeros_like(low[:, :HALF])
    top = np.concatenate([high[:, :HALF], high[:, :HALF], high[:, HALF:], high[:, HALF:]], axis=1)
    bottom = np.concatenate([low[:, :HALF], zero, low[:, HALF:], zero], axis=1)
    return np.concatenate([top, bottom], axis=0)


def far(n):
    return sorted(range(1, n), key=lambda d: -min(d, n - d))


def split(value):
    high = value.astype(BF)
    return high, (value - high.astype(F32)).astype(BF)


def dot(a, b):
    return lax.dot_general(a, b, (((1,), (0,)), ((), ())), preferred_element_type=F32)


def dot_t(a, b):
    return lax.dot_general(a, b, (((1,), (1,)), ((), ())), preferred_element_type=F32)


def lanes(shape, axis=1):
    return lax.broadcasted_iota(jnp.int32, shape, axis)


def kernel(
    nz,
    total_rows,
    snap_hbm,
    weight_hbm,
    start_hbm,
    table_hbm,
    gram_out,
    modes_out,
    weight_ref,
    start_ref,
    table_ref,
    x_ref,
    xc_ref,
    q_ref,
    ah_ref,
    al_ref,
    gs_ref,
    gr_ref,
    vs_ref,
    vx_ref,
    gx_ref,
    gy_ref,
    gz_ref,
    gf_ref,
    vy_ref,
    vz_ref,
    e_ref,
    ms_ref,
    mr_ref,
    sa_ref,
    sb_ref,
    small_sem,
    load_sem,
    gx_s,
    gx_r,
    gy_s,
    gy_r,
    gz_s,
    gz_r,
    ga_s,
    ga_r,
    vx_s,
    vx_r,
    vy_s,
    vy_r,
    vz_s,
    vz_r,
    e_s,
    e_r,
    m_s,
    m_r,
):
    halves = x_ref.shape[0] // HALF
    rows = x_ref.shape[1]
    pts = lax.axis_index("pts")
    me = lax.axis_index("freq")
    zc = pts // NY
    yc = pts % NY
    xc = me // 2
    core = me % 2

    chunks = load_sem.shape[0]
    span = x_ref.shape[0] // chunks

    def load(i):
        part = pl.ds(i * span, span)
        return pltpu.make_async_copy(snap_hbm.at[part, :], x_ref.at[part, :], load_sem.at[i])

    small = [
        pltpu.make_async_copy(source, target, small_sem.at[i])
        for i, (source, target) in enumerate(
            ((start_hbm, start_ref), (weight_hbm, weight_ref), (table_hbm, table_ref))
        )
    ]
    for copy in small[:2]:
        copy.start()
    for i in range(chunks):
        load(i).start()
    small[2].start()

    def freq_peer(i):
        step = (2, 1, 3, 0)[i // 2]
        return ((xc + step) % (NC // 2)) * 2 + (core + 1 - i % 2) % 2

    barrier = pltpu.get_barrier_semaphore()
    for i in range(NC - 1):
        pl.semaphore_signal(barrier, inc=1, device_id={"freq": freq_peer(i)}, device_id_type=MESH)
    for d in far(NY):
        pl.semaphore_signal(
            barrier, inc=1, device_id={"pts": zc * NY + (yc + d) % NY}, device_id_type=MESH
        )
    for d in far(nz):
        pl.semaphore_signal(
            barrier, inc=1, device_id={"pts": (zc + d) % nz * NY + yc}, device_id_type=MESH
        )

    small[0].wait()
    small[1].wait()

    groups = rows // 128
    weight = jnp.concatenate(
        [weight_ref[pl.ds(me * groups + j, 1), :] for j in range(groups)], axis=1
    )
    root = jnp.sqrt(weight)
    inv_root = 1.0 / root
    seg = lanes((NB, 128)) // 32
    coeffs = jnp.concatenate([start_ref[0], start_ref[1]], axis=1)

    for i in range(NF // 4):
        for odd in range(2):
            r1, r2, i1, i2 = (
                jnp.broadcast_to(coeffs[:, n : n + 1], (NB, 128))
                for n in (4 * i + 2 * odd, 4 * i + 2 * odd + 1, NF + 4 * i + 2 * odd, NF + 4 * i + 2 * odd + 1)
            )
            pair = 2 * i + odd
            sa_ref[pair] = jnp.where(seg == 0, r1, jnp.where(seg == 1, i1, jnp.where(seg == 2, r2, i2)))
            sb_ref[pair] = jnp.where(seg == 0, i1, jnp.where(seg == 1, -r1, jnp.where(seg == 2, i2, -r2)))

    total = jnp.zeros((24, rows), F32)
    for i in range(chunks):
        load(i).wait()
        for j in range(span // 24):
            total = total + x_ref[i * span + j * 24 : i * span + (j + 1) * 24, :]
    mean = jnp.sum(total, axis=0, keepdims=True) * (1.0 / x_ref.shape[0])

    small[2].wait()

    def centre(j):
        high, low = split((x_ref[j * HALF : (j + 1) * HALF, :] - mean) * root)
        xc_ref[j * NFFT : j * NFFT + HALF, :] = high
        xc_ref[j * NFFT + HALF : (j + 1) * NFFT, :] = low

    done = 0
    for b in range(0, NB, 2):
        while done < min(b + 3 + 2, halves):
            centre(done)
            done += 1
        right = jnp.concatenate(
            [xc_ref[n * NFFT : (n + 2) * NFFT, :] for n in (b, b + 1)], axis=1
        )
        both = dot(table_ref[...], right)
        value = both[: 2 * NF] + both[2 * NF :]
        for m in range(2):
            for j in range(groups):
                at = m * rows + j * 128
                q_ref[j, pl.ds(b + m, 2 * NF, stride=PITCH), :] = value[:, at : at + 128]


    per = NF // NC
    block = per * 2 * NB

    def gram_copy(to, slot):
        return pltpu.make_async_remote_copy(
            src_ref=gs_ref.at[to],
            dst_ref=gr_ref.at[slot],
            send_sem=gx_s.at[to],
            recv_sem=gx_r.at[slot],
            device_id={"freq": to},
            device_id_type=MESH,
        )

    def vx_copy(to, slot):
        return pltpu.make_async_remote_copy(
            src_ref=vs_ref.at[to],
            dst_ref=vx_ref.at[slot],
            send_sem=vx_s.at[to],
            recv_sem=vx_r.at[slot],
            device_id={"freq": to},
            device_id_type=MESH,
        )

    upper = lanes((NB, 128), 0) <= lanes((NB, 128)) % 32
    lane4 = lanes((per // 2, 128))
    lane = lanes((NB, 128))

    order = [freq_peer(i) for i in range(NC - 1)] + [me]

    def split_of(slot, p):
        for n in range(4):
            source = (order[slot] * (2 * per) + p * 4 + n) * PITCH
            value = [q_ref[j, pl.ds(source, NB), :] for j in range(groups)]
            high, low = split(jnp.concatenate(value, axis=1))
            at = slot * block + p * 128 + n * NB
            ah_ref[at : at + NB, :] = high
            al_ref[at : at + NB, :] = low

    def pair_gram(slot, p):
        at = slot * block + p * 128
        high = ah_ref[at : at + 128, :]
        out = dot_t(high, jnp.concatenate([high, al_ref[at : at + 128, :]], axis=0))
        cross = out[:, 128:]
        z = out[:, :128] + (cross + cross.T)
        r1, i1, r2, i2 = (z[n * NB : (n + 1) * NB] for n in range(4))
        even = jnp.where(lane < 64, r1, r2)
        odd = jnp.where(lane < 64, i1, i2)
        return jnp.where(
            seg % 2 == 0, even + pltpu.roll(odd, 96, 1), even - pltpu.roll(odd, 32, 1)
        )

    def gram_of(slot):
        owner = order[slot]
        parts_a, parts_b, packed = [], [], None
        for p in range(per // 2):
            g = pair_gram(slot, p)
            if slot + 1 < NC:
                split_of(slot + 1, p)
            pair = owner * (per // 2) + p
            parts_a.append(jnp.sum(g * sa_ref[pair], axis=0, keepdims=True))
            parts_b.append(jnp.sum(g * sb_ref[pair], axis=0, keepdims=True))
            if p % 2 == 0:
                packed = jnp.where(upper, g, pltpu.roll(g, 96, 1))
            else:
                half = jnp.where(upper, pltpu.roll(g, 32, 1), g)
                both = jnp.where(seg % 2 == 0, packed, half)
                gs_ref[owner, pl.ds(p // 2 * NB, NB), :] = both
        va = jnp.concatenate(parts_a, axis=0)
        vb = jnp.concatenate(parts_b, axis=0)
        vs_ref[owner] = jnp.where(
            lane4 // 32 % 2 == 0, va + pltpu.roll(va, 96, 1), vb + pltpu.roll(vb, 32, 1)
        )

    for p in range(per // 2):
        split_of(0, p)
    for slot in range(NC):
        gram_of(slot)
        if slot == 0:
            pl.semaphore_wait(barrier, NC - 1 + NY - 1 + nz - 1)
        if slot < NC - 1:
            vx_copy(order[slot], me).start()
            gram_copy(order[slot], me).start()
    vx_ref[me] = vs_ref[me]
    gr_ref[me] = gs_ref[me]

    def total_of(buf, n):
        out = buf[0]
        for i in range(1, n):
            out = out + buf[i]
        return out

    for i in range(NC - 1):
        sender = freq_peer(i)
        vx_copy(sender, sender).wait_recv()
    vy_ref[yc] = total_of(vx_ref, NC)

    gsub = gx_ref.shape[0] // NY

    def y_dev(other):
        return {"pts": zc * NY + other}

    def z_dev(other):
        return {"pts": other * NY + yc}

    def spread(buf, ssem, rsem, mine, other, device):
        return pltpu.make_async_remote_copy(
            src_ref=buf.at[mine],
            dst_ref=buf.at[mine],
            send_sem=ssem.at[other],
            recv_sem=rsem.at[mine],
            device_id=device,
            device_id_type=MESH,
        )

    def arrival(buf, ssem, rsem, other, device):
        return pltpu.make_async_remote_copy(
            src_ref=buf.at[other],
            dst_ref=buf.at[other],
            send_sem=ssem.at[other],
            recv_sem=rsem.at[other],
            device_id=device,
            device_id_type=MESH,
        )

    for d in far(NY):
        other = (yc + d) % NY
        spread(vy_ref, vy_s, vy_r, yc, other, y_dev(other)).start()

    for i in range(NC - 1):
        sender = freq_peer(i)
        gram_copy(sender, sender).wait_recv()
    gx_ref[...] = total_of(gr_ref, NC)

    def gram_y(other, slot):
        return pltpu.make_async_remote_copy(
            src_ref=gx_ref.at[pl.ds(pl.multiple_of(other * gsub, gsub), gsub), :],
            dst_ref=gy_ref.at[slot],
            send_sem=gy_s.at[other],
            recv_sem=gy_r.at[slot],
            device_id=y_dev(other),
            device_id_type=MESH,
        )

    for d in far(NY):
        gram_y((yc + d) % NY, yc).start()
    gy_ref[yc] = gx_ref[pl.ds(pl.multiple_of(yc * gsub, gsub), gsub), :]

    for d in far(NY):
        other = (yc + d) % NY
        arrival(vy_ref, vy_s, vy_r, other, y_dev(other)).wait_recv()
    vz_ref[zc] = total_of(vy_ref, NY)
    for d in far(nz):
        other = (zc + d) % nz
        spread(vz_ref, vz_s, vz_r, zc, other, z_dev(other)).start()

    for d in far(NY):
        other = (yc + d) % NY
        gram_y(other, other).wait_recv()
    gz_ref[zc] = total_of(gy_ref, NY)
    for d in far(nz):
        other = (zc + d) % nz
        spread(gz_ref, gz_s, gz_r, zc, other, z_dev(other)).start()

    for d in far(nz):
        other = (zc + d) % nz
        arrival(vz_ref, vz_s, vz_r, other, z_dev(other)).wait_recv()
    v = total_of(vz_ref, nz) * (1.0 / total_rows)

    square = v * v
    norm1 = jnp.sum(jnp.where(lane4 < 64, square, 0.0), axis=1, keepdims=True) * (1.0 / NB)
    norm2 = jnp.sum(jnp.where(lane4 >= 64, square, 0.0), axis=1, keepdims=True) * (1.0 / NB)
    y = v * (1.0 / jnp.sqrt(jnp.where(lane4 < 64, norm1, norm2) + 1e-06))
    turned = pltpu.roll(y, 64, 1)
    e_ref[me] = jnp.concatenate(
        [jnp.where(lane4 < 64, y, turned), jnp.where(lane4 < 64, turned, y)], axis=0
    )

    for i in range(NC - 1):
        to = freq_peer(i)
        spread(e_ref, e_s, e_r, me, to, {"freq": to}).start()

    line = lanes((2 * per, block), 0)
    own = lanes((2 * per, block)) // 64 == line % (per // 2) * 2 + line % per // (per // 2)
    sign = jnp.where(lanes((per, 128)) // 32 % 2 == 0, 1.0, -1.0)

    def project(slot):
        y = e_ref[order[slot]]
        e = jnp.concatenate([y * sign, pltpu.roll(y, 32, 1)], axis=0)
        left = jnp.where(own, jnp.concatenate([e] * (block // 128), axis=1), 0.0)
        high, low = split(left)
        first = slot * block
        right = ah_ref[first : first + block, :]
        both = dot(jnp.concatenate([high, low], axis=0), right)
        out = both[: 2 * per] + both[2 * per :] + dot(high, al_ref[first : first + block, :])
        return out * inv_root

    mr_ref[me] = project(NC - 1)

    for d in far(nz):
        other = (zc + d) % nz
        arrival(gz_ref, gz_s, gz_r, other, z_dev(other)).wait_recv()
    gf_ref[yc] = total_of(gz_ref, nz) * (1.0 / total_rows)
    for d in far(NY):
        other = (yc + d) % NY
        spread(gf_ref, ga_s, ga_r, yc, other, y_dev(other)).start()

    def modes_copy(to, slot):
        return pltpu.make_async_remote_copy(
            src_ref=ms_ref.at[to],
            dst_ref=mr_ref.at[slot],
            send_sem=m_s.at[to],
            recv_sem=m_r.at[slot],
            device_id={"freq": to},
            device_id_type=MESH,
        )

    for step in ((6,), (2, 3), (4, 5), (0, 1)):
        owners = [freq_peer(i) for i in step]
        for owner in owners:
            arrival(e_ref, e_s, e_r, owner, {"freq": owner}).wait_recv()
        values = [project(i) for i in step]
        for owner, value in zip(owners, values):
            ms_ref[owner] = value
        for owner in owners:
            modes_copy(owner, me).start()

    for d in far(NY):
        other = (yc + d) % NY
        arrival(gf_ref, ga_s, ga_r, other, y_dev(other)).wait_recv()
    for i in range(NY):
        gram_out[i * gsub : (i + 1) * gsub, :] = gf_ref[i]

    for i in range(NC - 1):
        to = freq_peer(i)
        gram_copy(to, me).wait_send()
        vx_copy(to, me).wait_send()
        spread(e_ref, e_s, e_r, me, to, {"freq": to}).wait_send()
    for d in far(NY):
        other = (yc + d) % NY
        spread(vy_ref, vy_s, vy_r, yc, other, y_dev(other)).wait_send()
        gram_y(other, yc).wait_send()
        spread(gf_ref, ga_s, ga_r, yc, other, y_dev(other)).wait_send()
    for d in far(nz):
        other = (zc + d) % nz
        spread(vz_ref, vz_s, vz_r, zc, other, z_dev(other)).wait_send()
        spread(gz_ref, gz_s, gz_r, zc, other, z_dev(other)).wait_send()

    for i in (6, 2, 3, 4, 5, 0, 1):
        sender = freq_peer(i)
        modes_copy(sender, sender).wait_recv()
    for s in range(NC):
        modes_out[s] = mr_ref[s]
    for i in range(NC - 1):
        modes_copy(freq_peer(i), me).wait_send()


def finish(gram_ref, modes_ref, gram_out, modes_out):
    rows = modes_ref.shape[2]
    per = modes_ref.shape[1] // 2
    for s in range(NC):
        value = modes_ref[s]
        for k in range(per):
            for c in range(2):
                line = c * per + k % 2 * (per // 2) + k // 2
                modes_out[k, c : c + 1, s * rows : (s + 1) * rows] = value[line : line + 1]
    packed = gram_ref[...]
    flipped = jnp.concatenate([packed, packed], axis=0).T
    above = lanes((NB, NB), 0) <= lanes((NB, NB))
    same = lanes((NB, NB), 0) == lanes((NB, NB))
    for q in range(per // 4):
        for k in range(4):
            here = packed[q * NB : (q + 1) * NB]
            there = flipped[k * NB : (k + 1) * NB]
            here = here if k == 0 else pltpu.roll(here, 128 - 32 * k, 1)
            there = there if q == 0 else pltpu.roll(there, 128 - 32 * q, 1)
            here, there = here[:, :NB], there[:, :NB]
            freq = 4 * q + (0, 2, 1, 3)[k]
            gram_out[freq, 0] = jnp.where(above, here, there)
            gram_out[freq, 1] = jnp.where(same, 0.0, jnp.where(above, -there, here))


def shards(nz, table, snapshots, weight, start_vec):
    times, rows = snapshots.shape
    total_rows = weight.shape[0] * lax.axis_size("pts")
    per = NF // NC
    dma = pltpu.SemaphoreType.DMA
    vmem = pl.BlockSpec(memory_space=pltpu.VMEM)
    gram_rows = per // 4 * NB
    gram, modes = pl.pallas_call(
        functools.partial(kernel, nz, total_rows),
        out_shape=(
            jax.ShapeDtypeStruct((gram_rows, 128), F32),
            jax.ShapeDtypeStruct((NC, per * 2, rows), F32),
        ),
        in_specs=[pl.BlockSpec(memory_space=pltpu.HBM)] * 4,
        out_specs=(vmem, vmem),
        scratch_shapes=[
            pltpu.VMEM((weight.shape[0] // 128, 128), F32),
            pltpu.VMEM((2, NB, NF), F32),
            pltpu.VMEM(table.shape, BF),
            pltpu.VMEM((times, rows), F32),
            pltpu.VMEM((times * 2, rows), BF),
            pltpu.VMEM((rows // 128, NF * 2 * PITCH, 128), F32),
            pltpu.VMEM((NF * 2 * NB, rows), BF),
            pltpu.VMEM((NF * 2 * NB, rows), BF),
            pltpu.VMEM((NC, gram_rows, 128), F32),
            pltpu.VMEM((NC, gram_rows, 128), F32),
            pltpu.VMEM((NC, per // 2, 128), F32),
            pltpu.VMEM((NC, per // 2, 128), F32),
            pltpu.VMEM((gram_rows, 128), F32),
            pltpu.VMEM((NY, gram_rows // NY, 128), F32),
            pltpu.VMEM((nz, gram_rows // NY, 128), F32),
            pltpu.VMEM((NY, gram_rows // NY, 128), F32),
            pltpu.VMEM((NY, per // 2, 128), F32),
            pltpu.VMEM((nz, per // 2, 128), F32),
            pltpu.VMEM((NC, per, 128), F32),
            pltpu.VMEM((NC, per * 2, rows), F32),
            pltpu.VMEM((NC, per * 2, rows), F32),
            pltpu.VMEM((NF // 2, NB, 128), F32),
            pltpu.VMEM((NF // 2, NB, 128), F32),
            dma((3,)),
            dma((8,)),
            dma((NC,)),
            dma((NC,)),
            dma((NY,)),
            dma((NY,)),
            dma((nz,)),
            dma((nz,)),
            dma((NY,)),
            dma((NY,)),
            dma((NC,)),
            dma((NC,)),
            dma((NY,)),
            dma((NY,)),
            dma((nz,)),
            dma((nz,)),
            dma((NC,)),
            dma((NC,)),
            dma((NC,)),
            dma((NC,)),
        ],
        compiler_params=pltpu.CompilerParams(
            collective_id=0, has_side_effects=True, vmem_limit_bytes=40 * 1024 * 1024
        ),
        name="spod",
    )(
        *(
            pltpu.with_memory_space_constraint(a, pltpu.HBM)
            for a in (snapshots, weight.reshape(-1, 128), start_vec.transpose(1, 2, 0), jnp.asarray(table))
        )
    )
    return pl.pallas_call(
        finish,
        out_shape=(
            jax.ShapeDtypeStruct((per, 2, NB, NB), F32),
            jax.ShapeDtypeStruct((per, 2, NC * rows), F32),
        ),
        in_specs=[vmem, vmem],
        out_specs=(vmem, vmem),
        compiler_params=pltpu.CompilerParams(vmem_limit_bytes=16 * 1024 * 1024),
        name="finish",
    )(gram, modes)


def solution(mesh):
    placed = (P(None, ("pts", "freq")), P("pts"), P())
    nz = mesh.shape["pts"] // NY
    return jax.shard_map(
        functools.partial(shards, nz, dft_operand()),
        mesh=mesh,
        in_specs=placed,
        out_specs=(P("freq", None, None, None), P("freq", None, "pts")),
        check_vma=False,
    )
```

```python
import functools
import math

import jax
import jax.numpy as jnp
import numpy as np
from jax import lax
from jax.experimental import pallas as pl
from jax.experimental.pallas import tpu as pltpu
from jax.sharding import PartitionSpec as P

NFFT = 128
NB = 32
NF = 64
HALF = NFFT // 2
NC = 8
NY = 8
PITCH = NB + 1
MESH = pl.DeviceIdType.MESH
BF = jnp.bfloat16
F32 = jnp.float32


def dft_operand():
    times = np.arange(NFFT)
    phases = (np.arange(NF)[:, None] * times[None, :] % NFFT) * (2.0 * math.pi / NFFT)
    window = 0.5 - 0.5 * np.cos(times * (2.0 * math.pi / NFFT))
    window = window / np.sqrt(np.sum(window * window))
    rows = np.stack([np.cos(phases) * window, -np.sin(phases) * window], axis=1)
    rows = rows.reshape(2 * NF, NFFT).astype(np.float32)
    steady = [float(np.sum(rows[n], dtype=np.float64)) for n in (0, 2)]
    high = rows.astype(BF)
    low = (rows - high.astype(np.float32)).astype(BF)
    zero = np.zeros_like(low[:, :HALF])
    top = np.concatenate([high[:, :HALF], high[:, :HALF], high[:, HALF:], high[:, HALF:]], axis=1)
    bottom = np.concatenate([low[:, :HALF], zero, low[:, HALF:], zero], axis=1)
    return np.concatenate([top, bottom], axis=0), steady


def far(n):
    return sorted(range(1, n), key=lambda d: -min(d, n - d))


def split(value):
    high = value.astype(BF)
    return high, (value - high.astype(F32)).astype(BF)


def dot(a, b):
    return lax.dot_general(a, b, (((1,), (0,)), ((), ())), preferred_element_type=F32)


def dot_t(a, b):
    return lax.dot_general(a, b, (((1,), (1,)), ((), ())), preferred_element_type=F32)


def lanes(shape, axis=1):
    return lax.broadcasted_iota(jnp.int32, shape, axis)


def kernel(
    nz,
    total_rows,
    steady,
    snap_hbm,
    weight_hbm,
    start_hbm,
    table_hbm,
    gram_out,
    modes_out,
    weight_ref,
    start_ref,
    table_ref,
    x_ref,
    xc_ref,
    q_ref,
    ah_ref,
    al_ref,
    gs_ref,
    gr_ref,
    vs_ref,
    vx_ref,
    gx_ref,
    gy_ref,
    gz_ref,
    gf_ref,
    vy_ref,
    vz_ref,
    e_ref,
    ms_ref,
    mr_ref,
    sa_ref,
    sb_ref,
    small_sem,
    load_sem,
    gx_s,
    gx_r,
    gy_s,
    gy_r,
    gz_s,
    gz_r,
    ga_s,
    ga_r,
    vx_s,
    vx_r,
    vy_s,
    vy_r,
    vz_s,
    vz_r,
    e_s,
    e_r,
    m_s,
    m_r,
):
    halves = x_ref.shape[0] // HALF
    rows = x_ref.shape[1]
    pts = lax.axis_index("pts")
    me = lax.axis_index("freq")
    zc = pts // NY
    yc = pts % NY
    xc = me // 2
    core = me % 2

    bounds = [0, 17, halves]

    def load(i):
        part = pl.ds(bounds[i] * HALF, (bounds[i + 1] - bounds[i]) * HALF)
        return pltpu.make_async_copy(snap_hbm.at[part, :], x_ref.at[part, :], load_sem.at[i])

    small = [
        pltpu.make_async_copy(source, target, small_sem.at[i])
        for i, (source, target) in enumerate(
            ((start_hbm, start_ref), (weight_hbm, weight_ref), (table_hbm, table_ref))
        )
    ]
    for copy in small[:2]:
        copy.start()
    load(0).start()
    small[2].start()
    for i in range(1, len(bounds) - 1):
        load(i).start()

    def freq_peer(i):
        step = (2, 1, 3, 0)[i // 2]
        return ((xc + step) % (NC // 2)) * 2 + (core + 1 - i % 2) % 2

    barrier = pltpu.get_barrier_semaphore()
    for i in range(NC - 1):
        pl.semaphore_signal(barrier, inc=1, device_id={"freq": freq_peer(i)}, device_id_type=MESH)
    for d in far(NY):
        pl.semaphore_signal(
            barrier, inc=1, device_id={"pts": zc * NY + (yc + d) % NY}, device_id_type=MESH
        )
    for d in far(nz):
        pl.semaphore_signal(
            barrier, inc=1, device_id={"pts": (zc + d) % nz * NY + yc}, device_id_type=MESH
        )

    small[0].wait()
    small[1].wait()

    groups = rows // 128
    weight = jnp.concatenate(
        [weight_ref[pl.ds(me * groups + j, 1), :] for j in range(groups)], axis=1
    )
    root = jnp.sqrt(weight)
    inv_root = 1.0 / root
    seg = lanes((NB, 128)) // 32
    coeffs = jnp.concatenate([start_ref[0], start_ref[1]], axis=1)

    def coefficient_tables(i):
        for odd in range(2):
            r1, r2, i1, i2 = (
                jnp.broadcast_to(coeffs[:, n : n + 1], (NB, 128))
                for n in (4 * i + 2 * odd, 4 * i + 2 * odd + 1, NF + 4 * i + 2 * odd, NF + 4 * i + 2 * odd + 1)
            )
            pair = 2 * i + odd
            sa_ref[pair] = jnp.where(seg == 0, r1, jnp.where(seg == 1, i1, jnp.where(seg == 2, r2, i2)))
            sb_ref[pair] = jnp.where(seg == 0, i1, jnp.where(seg == 1, -r1, jnp.where(seg == 2, i2, -r2)))

    def sum_of(first, last):
        out = x_ref[first * HALF : first * HALF + 32, :]
        for n in range(first * HALF + 32, last * HALF, 32):
            out = out + x_ref[n : n + 32, :]
        return out

    for i in range(12):
        coefficient_tables(i)

    load(0).wait()
    total = sum_of(0, bounds[1])
    about = jnp.sum(total, axis=0, keepdims=True) * (1.0 / (bounds[1] * HALF))

    def centre(j):
        high, low = split((x_ref[j * HALF : (j + 1) * HALF, :] - about) * root)
        xc_ref[j * NFFT : j * NFFT + HALF, :] = high
        xc_ref[j * NFFT + HALF : (j + 1) * NFFT, :] = low

    small[2].wait()
    done = 0
    for chunk in range(len(bounds) - 1):
        if chunk:
            load(chunk).wait()
        for b in range(max(bounds[chunk] - 1, 0), bounds[chunk + 1] - 1, 2):
            while done < min(b + 5, bounds[chunk + 1]):
                centre(done)
                done += 1
            right = jnp.concatenate(
                [xc_ref[n * NFFT : (n + 2) * NFFT, :] for n in (b, b + 1)], axis=1
            )
            both = dot(table_ref[...], right)
            value = both[: 2 * NF] + both[2 * NF :]
            for m in range(2):
                for j in range(groups):
                    at = m * rows + j * 128
                    q_ref[j, pl.ds(b + m, 2 * NF, stride=PITCH), :] = value[:, at : at + 128]
        if chunk:
            total = total + sum_of(bounds[chunk], bounds[chunk + 1])
        if chunk == 1:
            for i in range(12, NF // 4):
                coefficient_tables(i)

    mean = jnp.sum(total, axis=0, keepdims=True) * (1.0 / x_ref.shape[0])
    shift = (mean - about) * root
    for k, constant in enumerate(steady):
        at = 2 * k * PITCH
        for j in range(groups):
            q_ref[j, at : at + NB, :] -= constant * shift[:, j * 128 : (j + 1) * 128]

    per = NF // NC
    block = per * 2 * NB

    def gram_copy(to, slot):
        return pltpu.make_async_remote_copy(
            src_ref=gs_ref.at[to],
            dst_ref=gr_ref.at[slot],
            send_sem=gx_s.at[to],
            recv_sem=gx_r.at[slot],
            device_id={"freq": to},
            device_id_type=MESH,
        )

    def vx_copy(to, slot):
        return pltpu.make_async_remote_copy(
            src_ref=vs_ref.at[to],
            dst_ref=vx_ref.at[slot],
            send_sem=vx_s.at[to],
            recv_sem=vx_r.at[slot],
            device_id={"freq": to},
            device_id_type=MESH,
        )

    upper = lanes((NB, 128), 0) <= lanes((NB, 128)) % 32
    lane4 = lanes((per // 2, 128))
    lane = lanes((NB, 128))

    order = [freq_peer(i) for i in range(NC - 1)] + [me]

    def split_of(slot, p):
        for n in range(4):
            source = (order[slot] * (2 * per) + p * 4 + n) * PITCH
            value = [q_ref[j, pl.ds(source, NB), :] for j in range(groups)]
            high, low = split(jnp.concatenate(value, axis=1))
            at = slot * block + p * 128 + n * NB
            ah_ref[at : at + NB, :] = high
            al_ref[at : at + NB, :] = low

    def pair_gram(slot, p):
        at = slot * block + p * 128
        high = ah_ref[at : at + 128, :]
        out = dot_t(high, jnp.concatenate([high, al_ref[at : at + 128, :]], axis=0))
        cross = out[:, 128:]
        z = out[:, :128] + (cross + cross.T)
        r1, i1, r2, i2 = (z[n * NB : (n + 1) * NB] for n in range(4))
        even = jnp.where(lane < 64, r1, r2)
        odd = jnp.where(lane < 64, i1, i2)
        return jnp.where(
            seg % 2 == 0, even + pltpu.roll(odd, 96, 1), even - pltpu.roll(odd, 32, 1)
        )

    def gram_of(slot):
        owner = order[slot]
        parts_a, parts_b, packed = [], [], None
        for p in range(per // 2):
            g = pair_gram(slot, p)
            if slot + 1 < NC:
                split_of(slot + 1, p)
            pair = owner * (per // 2) + p
            parts_a.append(jnp.sum(g * sa_ref[pair], axis=0, keepdims=True))
            parts_b.append(jnp.sum(g * sb_ref[pair], axis=0, keepdims=True))
            if p % 2 == 0:
                packed = jnp.where(upper, g, pltpu.roll(g, 96, 1))
            else:
                half = jnp.where(upper, pltpu.roll(g, 32, 1), g)
                both = jnp.where(seg % 2 == 0, packed, half)
                gs_ref[owner, pl.ds(p // 2 * NB, NB), :] = both
        va = jnp.concatenate(parts_a, axis=0)
        vb = jnp.concatenate(parts_b, axis=0)
        vs_ref[owner] = jnp.where(
            lane4 // 32 % 2 == 0, va + pltpu.roll(va, 96, 1), vb + pltpu.roll(vb, 32, 1)
        )

    for p in range(per // 2):
        split_of(0, p)
    for slot in range(NC):
        gram_of(slot)
        if slot == 0:
            pl.semaphore_wait(barrier, NC - 1 + NY - 1 + nz - 1)
        if slot < NC - 1:
            vx_copy(order[slot], me).start()
            gram_copy(order[slot], me).start()
    vx_ref[me] = vs_ref[me]
    gr_ref[me] = gs_ref[me]

    def total_of(buf, n):
        out = buf[0]
        for i in range(1, n):
            out = out + buf[i]
        return out

    for i in range(NC - 1):
        sender = freq_peer(i)
        vx_copy(sender, sender).wait_recv()
    vy_ref[yc] = total_of(vx_ref, NC)

    gsub = gx_ref.shape[0] // NY

    def y_dev(other):
        return {"pts": zc * NY + other}

    def z_dev(other):
        return {"pts": other * NY + yc}

    def spread(buf, ssem, rsem, mine, other, device):
        return pltpu.make_async_remote_copy(
            src_ref=buf.at[mine],
            dst_ref=buf.at[mine],
            send_sem=ssem.at[other],
            recv_sem=rsem.at[mine],
            device_id=device,
            device_id_type=MESH,
        )

    def arrival(buf, ssem, rsem, other, device):
        return pltpu.make_async_remote_copy(
            src_ref=buf.at[other],
            dst_ref=buf.at[other],
            send_sem=ssem.at[other],
            recv_sem=rsem.at[other],
            device_id=device,
            device_id_type=MESH,
        )

    for d in far(NY):
        other = (yc + d) % NY
        spread(vy_ref, vy_s, vy_r, yc, other, y_dev(other)).start()

    for i in range(NC - 1):
        sender = freq_peer(i)
        gram_copy(sender, sender).wait_recv()
    gx_ref[...] = total_of(gr_ref, NC)

    def gram_y(other, slot):
        return pltpu.make_async_remote_copy(
            src_ref=gx_ref.at[pl.ds(pl.multiple_of(other * gsub, gsub), gsub), :],
            dst_ref=gy_ref.at[slot],
            send_sem=gy_s.at[other],
            recv_sem=gy_r.at[slot],
            device_id=y_dev(other),
            device_id_type=MESH,
        )

    for d in far(NY):
        gram_y((yc + d) % NY, yc).start()
    gy_ref[yc] = gx_ref[pl.ds(pl.multiple_of(yc * gsub, gsub), gsub), :]

    for d in far(NY):
        other = (yc + d) % NY
        arrival(vy_ref, vy_s, vy_r, other, y_dev(other)).wait_recv()
    vz_ref[zc] = total_of(vy_ref, NY)
    for d in far(nz):
        other = (zc + d) % nz
        spread(vz_ref, vz_s, vz_r, zc, other, z_dev(other)).start()

    for d in far(NY):
        other = (yc + d) % NY
        gram_y(other, other).wait_recv()
    gz_ref[zc] = total_of(gy_ref, NY)
    for d in far(nz):
        other = (zc + d) % nz
        spread(gz_ref, gz_s, gz_r, zc, other, z_dev(other)).start()

    for d in far(nz):
        other = (zc + d) % nz
        arrival(vz_ref, vz_s, vz_r, other, z_dev(other)).wait_recv()
    v = total_of(vz_ref, nz) * (1.0 / total_rows)

    square = v * v
    norm1 = jnp.sum(jnp.where(lane4 < 64, square, 0.0), axis=1, keepdims=True) * (1.0 / NB)
    norm2 = jnp.sum(jnp.where(lane4 >= 64, square, 0.0), axis=1, keepdims=True) * (1.0 / NB)
    y = v * (1.0 / jnp.sqrt(jnp.where(lane4 < 64, norm1, norm2) + 1e-06))
    turned = pltpu.roll(y, 64, 1)
    e_ref[me] = jnp.concatenate(
        [jnp.where(lane4 < 64, y, turned), jnp.where(lane4 < 64, turned, y)], axis=0
    )

    for i in range(NC - 1):
        to = freq_peer(i)
        spread(e_ref, e_s, e_r, me, to, {"freq": to}).start()

    line = lanes((2 * per, block), 0)
    own = lanes((2 * per, block)) // 64 == line % (per // 2) * 2 + line % per // (per // 2)
    sign = jnp.where(lanes((per, 128)) // 32 % 2 == 0, 1.0, -1.0)

    def project(slot):
        y = e_ref[order[slot]]
        e = jnp.concatenate([y * sign, pltpu.roll(y, 32, 1)], axis=0)
        left = jnp.where(own, jnp.concatenate([e] * (block // 128), axis=1), 0.0)
        high, low = split(left)
        first = slot * block
        right = ah_ref[first : first + block, :]
        both = dot(jnp.concatenate([high, low], axis=0), right)
        out = both[: 2 * per] + both[2 * per :] + dot(high, al_ref[first : first + block, :])
        return out * inv_root

    mr_ref[me] = project(NC - 1)

    for d in far(nz):
        other = (zc + d) % nz
        arrival(gz_ref, gz_s, gz_r, other, z_dev(other)).wait_recv()
    gf_ref[yc] = total_of(gz_ref, nz) * (1.0 / total_rows)
    for d in far(NY):
        other = (yc + d) % NY
        spread(gf_ref, ga_s, ga_r, yc, other, y_dev(other)).start()

    def modes_copy(to, slot):
        return pltpu.make_async_remote_copy(
            src_ref=ms_ref.at[to],
            dst_ref=mr_ref.at[slot],
            send_sem=m_s.at[to],
            recv_sem=m_r.at[slot],
            device_id={"freq": to},
            device_id_type=MESH,
        )

    for step in ((6,), (2, 3), (4, 5), (0, 1)):
        owners = [freq_peer(i) for i in step]
        for owner in owners:
            arrival(e_ref, e_s, e_r, owner, {"freq": owner}).wait_recv()
        values = [project(i) for i in step]
        for owner, value in zip(owners, values):
            ms_ref[owner] = value
        for owner in owners:
            modes_copy(owner, me).start()

    for d in far(NY):
        other = (yc + d) % NY
        arrival(gf_ref, ga_s, ga_r, other, y_dev(other)).wait_recv()
    for i in range(NY):
        gram_out[i * gsub : (i + 1) * gsub, :] = gf_ref[i]

    for i in range(NC - 1):
        to = freq_peer(i)
        gram_copy(to, me).wait_send()
        vx_copy(to, me).wait_send()
        spread(e_ref, e_s, e_r, me, to, {"freq": to}).wait_send()
    for d in far(NY):
        other = (yc + d) % NY
        spread(vy_ref, vy_s, vy_r, yc, other, y_dev(other)).wait_send()
        gram_y(other, yc).wait_send()
        spread(gf_ref, ga_s, ga_r, yc, other, y_dev(other)).wait_send()
    for d in far(nz):
        other = (zc + d) % nz
        spread(vz_ref, vz_s, vz_r, zc, other, z_dev(other)).wait_send()
        spread(gz_ref, gz_s, gz_r, zc, other, z_dev(other)).wait_send()

    for i in (6, 2, 3, 4, 5, 0, 1):
        sender = freq_peer(i)
        modes_copy(sender, sender).wait_recv()
    for s in range(NC):
        modes_out[s] = mr_ref[s]
    for i in range(NC - 1):
        modes_copy(freq_peer(i), me).wait_send()


def finish(gram_ref, modes_ref, gram_out, modes_out):
    rows = modes_ref.shape[2]
    per = modes_ref.shape[1] // 2
    for s in range(NC):
        value = modes_ref[s]
        for k in range(per):
            for c in range(2):
                line = c * per + k % 2 * (per // 2) + k // 2
                modes_out[k, c : c + 1, s * rows : (s + 1) * rows] = value[line : line + 1]
    packed = gram_ref[...]
    flipped = jnp.concatenate([packed, packed], axis=0).T
    above = lanes((NB, NB), 0) <= lanes((NB, NB))
    same = lanes((NB, NB), 0) == lanes((NB, NB))
    for q in range(per // 4):
        for k in range(4):
            here = packed[q * NB : (q + 1) * NB]
            there = flipped[k * NB : (k + 1) * NB]
            here = here if k == 0 else pltpu.roll(here, 128 - 32 * k, 1)
            there = there if q == 0 else pltpu.roll(there, 128 - 32 * q, 1)
            here, there = here[:, :NB], there[:, :NB]
            freq = 4 * q + (0, 2, 1, 3)[k]
            gram_out[freq, 0] = jnp.where(above, here, there)
            gram_out[freq, 1] = jnp.where(same, 0.0, jnp.where(above, -there, here))


def shards(nz, tables, snapshots, weight, start_vec):
    times, rows = snapshots.shape
    table, steady = tables
    total_rows = weight.shape[0] * lax.axis_size("pts")
    per = NF // NC
    dma = pltpu.SemaphoreType.DMA
    vmem = pl.BlockSpec(memory_space=pltpu.VMEM)
    gram_rows = per // 4 * NB
    gram, modes = pl.pallas_call(
        functools.partial(kernel, nz, total_rows, steady),
        out_shape=(
            jax.ShapeDtypeStruct((gram_rows, 128), F32),
            jax.ShapeDtypeStruct((NC, per * 2, rows), F32),
        ),
        in_specs=[pl.BlockSpec(memory_space=pltpu.HBM)] * 4,
        out_specs=(vmem, vmem),
        scratch_shapes=[
            pltpu.VMEM((weight.shape[0] // 128, 128), F32),
            pltpu.VMEM((2, NB, NF), F32),
            pltpu.VMEM(table.shape, BF),
            pltpu.VMEM((times, rows), F32),
            pltpu.VMEM((times * 2, rows), BF),
            pltpu.VMEM((rows // 128, NF * 2 * PITCH, 128), F32),
            pltpu.VMEM((NF * 2 * NB, rows), BF),
            pltpu.VMEM((NF * 2 * NB, rows), BF),
            pltpu.VMEM((NC, gram_rows, 128), F32),
            pltpu.VMEM((NC, gram_rows, 128), F32),
            pltpu.VMEM((NC, per // 2, 128), F32),
            pltpu.VMEM((NC, per // 2, 128), F32),
            pltpu.VMEM((gram_rows, 128), F32),
            pltpu.VMEM((NY, gram_rows // NY, 128), F32),
            pltpu.VMEM((nz, gram_rows // NY, 128), F32),
            pltpu.VMEM((NY, gram_rows // NY, 128), F32),
            pltpu.VMEM((NY, per // 2, 128), F32),
            pltpu.VMEM((nz, per // 2, 128), F32),
            pltpu.VMEM((NC, per, 128), F32),
            pltpu.VMEM((NC, per * 2, rows), F32),
            pltpu.VMEM((NC, per * 2, rows), F32),
            pltpu.VMEM((NF // 2, NB, 128), F32),
            pltpu.VMEM((NF // 2, NB, 128), F32),
            dma((3,)),
            dma((2,)),
            dma((NC,)),
            dma((NC,)),
            dma((NY,)),
            dma((NY,)),
            dma((nz,)),
            dma((nz,)),
            dma((NY,)),
            dma((NY,)),
            dma((NC,)),
            dma((NC,)),
            dma((NY,)),
            dma((NY,)),
            dma((nz,)),
            dma((nz,)),
            dma((NC,)),
            dma((NC,)),
            dma((NC,)),
            dma((NC,)),
        ],
        compiler_params=pltpu.CompilerParams(
            collective_id=0, has_side_effects=True, vmem_limit_bytes=40 * 1024 * 1024
        ),
        name="spod",
    )(
        *(
            pltpu.with_memory_space_constraint(a, pltpu.HBM)
            for a in (snapshots, weight.reshape(-1, 128), start_vec.transpose(1, 2, 0), jnp.asarray(table))
        )
    )
    return pl.pallas_call(
        finish,
        out_shape=(
            jax.ShapeDtypeStruct((per, 2, NB, NB), F32),
            jax.ShapeDtypeStruct((per, 2, NC * rows), F32),
        ),
        in_specs=[vmem, vmem],
        out_specs=(vmem, vmem),
        compiler_params=pltpu.CompilerParams(vmem_limit_bytes=16 * 1024 * 1024),
        name="finish",
    )(gram, modes)


def solution(mesh):
    placed = (P(None, ("pts", "freq")), P("pts"), P())
    nz = mesh.shape["pts"] // NY
    return jax.shard_map(
        functools.partial(shards, nz, dft_operand()),
        mesh=mesh,
        in_specs=placed,
        out_specs=(P("freq", None, None, None), P("freq", None, "pts")),
        check_vma=False,
    )
```

```python
import functools
import math

import jax
import jax.numpy as jnp
import numpy as np
from jax import lax
from jax.experimental import pallas as pl
from jax.experimental.pallas import tpu as pltpu
from jax.sharding import PartitionSpec as P

NFFT = 128
NB = 32
NF = 64
HALF = NFFT // 2
NC = 8
NY = 8
PITCH = NB + 1
MESH = pl.DeviceIdType.MESH
BF = jnp.bfloat16
F32 = jnp.float32


def dft_operand():
    times = np.arange(NFFT)
    phases = (np.arange(NF)[:, None] * times[None, :] % NFFT) * (2.0 * math.pi / NFFT)
    window = 0.5 - 0.5 * np.cos(times * (2.0 * math.pi / NFFT))
    window = window / np.sqrt(np.sum(window * window))
    rows = np.stack([np.cos(phases) * window, -np.sin(phases) * window], axis=1)
    rows = rows.reshape(2 * NF, NFFT).astype(np.float32)
    steady = [float(np.sum(rows[n], dtype=np.float64)) for n in (0, 2)]
    high = rows.astype(BF)
    low = (rows - high.astype(np.float32)).astype(BF)
    zero = np.zeros_like(low[:, :HALF])
    top = np.concatenate([high[:, :HALF], high[:, :HALF], high[:, HALF:], high[:, HALF:]], axis=1)
    bottom = np.concatenate([low[:, :HALF], zero, low[:, HALF:], zero], axis=1)
    return np.concatenate([top, bottom], axis=0), steady


def far(n):
    return sorted(range(1, n), key=lambda d: -min(d, n - d))


def split(value):
    high = value.astype(BF)
    return high, (value - high.astype(F32)).astype(BF)


def dot(a, b):
    return lax.dot_general(a, b, (((1,), (0,)), ((), ())), preferred_element_type=F32)


def dot_t(a, b):
    return lax.dot_general(a, b, (((1,), (1,)), ((), ())), preferred_element_type=F32)


def lanes(shape, axis=1):
    return lax.broadcasted_iota(jnp.int32, shape, axis)


def kernel(
    nz,
    total_rows,
    steady,
    snap_hbm,
    weight_hbm,
    start_hbm,
    table_hbm,
    gram_out,
    modes_out,
    weight_ref,
    start_ref,
    table_ref,
    x_ref,
    xc_ref,
    q_ref,
    ah_ref,
    al_ref,
    gs_ref,
    gr_ref,
    vs_ref,
    vx_ref,
    gx_ref,
    gy_ref,
    gz_ref,
    gf_ref,
    vy_ref,
    vz_ref,
    e_ref,
    ms_ref,
    sa_ref,
    sb_ref,
    small_sem,
    load_sem,
    gx_s,
    gx_r,
    gy_s,
    gy_r,
    gz_s,
    gz_r,
    ga_s,
    ga_r,
    vx_s,
    vx_r,
    vy_s,
    vy_r,
    vz_s,
    vz_r,
    e_s,
    e_r,
    m_s,
    m_r,
):
    halves = x_ref.shape[0] // HALF
    rows = x_ref.shape[1]
    pts = lax.axis_index("pts")
    me = lax.axis_index("freq")
    zc = pts // NY
    yc = pts % NY
    xc = me // 2
    core = me % 2

    bounds = [0, 17, halves]

    def load(i):
        part = pl.ds(bounds[i] * HALF, (bounds[i + 1] - bounds[i]) * HALF)
        return pltpu.make_async_copy(snap_hbm.at[part, :], x_ref.at[part, :], load_sem.at[i])

    small = [
        pltpu.make_async_copy(source, target, small_sem.at[i])
        for i, (source, target) in enumerate(
            ((start_hbm, start_ref), (weight_hbm, weight_ref), (table_hbm, table_ref))
        )
    ]
    for copy in small[:2]:
        copy.start()
    load(0).start()
    small[2].start()
    for i in range(1, len(bounds) - 1):
        load(i).start()

    def freq_peer(i):
        step = (2, 1, 3, 0)[i // 2]
        return ((xc + step) % (NC // 2)) * 2 + (core + 1 - i % 2) % 2

    barrier = pltpu.get_barrier_semaphore()
    for i in range(NC - 1):
        pl.semaphore_signal(barrier, inc=1, device_id={"freq": freq_peer(i)}, device_id_type=MESH)
    for d in far(NY):
        pl.semaphore_signal(
            barrier, inc=1, device_id={"pts": zc * NY + (yc + d) % NY}, device_id_type=MESH
        )
    for d in far(nz):
        pl.semaphore_signal(
            barrier, inc=1, device_id={"pts": (zc + d) % nz * NY + yc}, device_id_type=MESH
        )

    small[0].wait()
    small[1].wait()

    groups = rows // 128
    weight = jnp.concatenate(
        [weight_ref[pl.ds(me * groups + j, 1), :] for j in range(groups)], axis=1
    )
    root = jnp.sqrt(weight)
    inv_root = 1.0 / root
    seg = lanes((NB, 128)) // 32
    coeffs = jnp.concatenate([start_ref[0], start_ref[1]], axis=1)

    def coefficient_tables(i):
        for odd in range(2):
            r1, r2, i1, i2 = (
                jnp.broadcast_to(coeffs[:, n : n + 1], (NB, 128))
                for n in (4 * i + 2 * odd, 4 * i + 2 * odd + 1, NF + 4 * i + 2 * odd, NF + 4 * i + 2 * odd + 1)
            )
            pair = 2 * i + odd
            sa_ref[pair] = jnp.where(seg == 0, r1, jnp.where(seg == 1, i1, jnp.where(seg == 2, r2, i2)))
            sb_ref[pair] = jnp.where(seg == 0, i1, jnp.where(seg == 1, -r1, jnp.where(seg == 2, i2, -r2)))

    def sum_of(first, last):
        out = x_ref[first * HALF : first * HALF + 32, :]
        for n in range(first * HALF + 32, last * HALF, 32):
            out = out + x_ref[n : n + 32, :]
        return out

    for i in range(12):
        coefficient_tables(i)

    load(0).wait()
    total = sum_of(0, bounds[1])
    about = jnp.sum(total, axis=0, keepdims=True) * (1.0 / (bounds[1] * HALF))

    def centre(j):
        high, low = split((x_ref[j * HALF : (j + 1) * HALF, :] - about) * root)
        xc_ref[j * NFFT : j * NFFT + HALF, :] = high
        xc_ref[j * NFFT + HALF : (j + 1) * NFFT, :] = low

    small[2].wait()
    done = 0
    for chunk in range(len(bounds) - 1):
        if chunk:
            load(chunk).wait()
        for b in range(max(bounds[chunk] - 1, 0), bounds[chunk + 1] - 1, 2):
            while done < min(b + 5, bounds[chunk + 1]):
                centre(done)
                done += 1
            right = jnp.concatenate(
                [xc_ref[n * NFFT : (n + 2) * NFFT, :] for n in (b, b + 1)], axis=1
            )
            both = dot(table_ref[...], right)
            value = both[: 2 * NF] + both[2 * NF :]
            for m in range(2):
                for j in range(groups):
                    at = m * rows + j * 128
                    q_ref[j, pl.ds(b + m, 2 * NF, stride=PITCH), :] = value[:, at : at + 128]
        if chunk:
            total = total + sum_of(bounds[chunk], bounds[chunk + 1])
        if chunk == 1:
            for i in range(12, NF // 4):
                coefficient_tables(i)

    mean = jnp.sum(total, axis=0, keepdims=True) * (1.0 / x_ref.shape[0])
    shift = (mean - about) * root
    for k, constant in enumerate(steady):
        at = 2 * k * PITCH
        for j in range(groups):
            q_ref[j, at : at + NB, :] -= constant * shift[:, j * 128 : (j + 1) * 128]

    per = NF // NC
    block = per * 2 * NB

    def gram_copy(to, slot):
        return pltpu.make_async_remote_copy(
            src_ref=gs_ref.at[to],
            dst_ref=gr_ref.at[slot],
            send_sem=gx_s.at[to],
            recv_sem=gx_r.at[slot],
            device_id={"freq": to},
            device_id_type=MESH,
        )

    def vx_copy(to, slot):
        return pltpu.make_async_remote_copy(
            src_ref=vs_ref.at[to],
            dst_ref=vx_ref.at[slot],
            send_sem=vx_s.at[to],
            recv_sem=vx_r.at[slot],
            device_id={"freq": to},
            device_id_type=MESH,
        )

    upper = lanes((NB, 128), 0) <= lanes((NB, 128)) % 32
    lane4 = lanes((per // 2, 128))
    lane = lanes((NB, 128))

    order = [freq_peer(i) for i in range(NC - 1)] + [me]

    def split_of(slot, p):
        for n in range(4):
            source = (order[slot] * (2 * per) + p * 4 + n) * PITCH
            value = [q_ref[j, pl.ds(source, NB), :] for j in range(groups)]
            high, low = split(jnp.concatenate(value, axis=1))
            at = slot * block + p * 128 + n * NB
            ah_ref[at : at + NB, :] = high
            al_ref[at : at + NB, :] = low

    def pair_gram(slot, p):
        at = slot * block + p * 128
        high = ah_ref[at : at + 128, :]
        out = dot_t(high, jnp.concatenate([high, al_ref[at : at + 128, :]], axis=0))
        cross = out[:, 128:]
        z = out[:, :128] + (cross + cross.T)
        r1, i1, r2, i2 = (z[n * NB : (n + 1) * NB] for n in range(4))
        even = jnp.where(lane < 64, r1, r2)
        odd = jnp.where(lane < 64, i1, i2)
        return jnp.where(
            seg % 2 == 0, even + pltpu.roll(odd, 96, 1), even - pltpu.roll(odd, 32, 1)
        )

    def gram_of(slot):
        owner = order[slot]
        parts_a, parts_b, packed = [], [], None
        for p in range(per // 2):
            g = pair_gram(slot, p)
            if slot + 1 < NC:
                split_of(slot + 1, p)
            pair = owner * (per // 2) + p
            parts_a.append(jnp.sum(g * sa_ref[pair], axis=0, keepdims=True))
            parts_b.append(jnp.sum(g * sb_ref[pair], axis=0, keepdims=True))
            if p % 2 == 0:
                packed = jnp.where(upper, g, pltpu.roll(g, 96, 1))
            else:
                half = jnp.where(upper, pltpu.roll(g, 32, 1), g)
                both = jnp.where(seg % 2 == 0, packed, half)
                gs_ref[owner, pl.ds(p // 2 * NB, NB), :] = both
        va = jnp.concatenate(parts_a, axis=0)
        vb = jnp.concatenate(parts_b, axis=0)
        vs_ref[owner] = jnp.where(
            lane4 // 32 % 2 == 0, va + pltpu.roll(va, 96, 1), vb + pltpu.roll(vb, 32, 1)
        )

    for p in range(per // 2):
        split_of(0, p)
    for slot in range(NC):
        gram_of(slot)
        if slot == 0:
            pl.semaphore_wait(barrier, NC - 1 + NY - 1 + nz - 1)
        if slot < NC - 1:
            vx_copy(order[slot], me).start()
            gram_copy(order[slot], me).start()
    vx_ref[me] = vs_ref[me]
    gr_ref[me] = gs_ref[me]

    def total_of(buf, n):
        out = buf[0]
        for i in range(1, n):
            out = out + buf[i]
        return out

    for i in range(NC - 1):
        sender = freq_peer(i)
        vx_copy(sender, sender).wait_recv()
    vy_ref[yc] = total_of(vx_ref, NC)

    gsub = gx_ref.shape[0] // NY

    def y_dev(other):
        return {"pts": zc * NY + other}

    def z_dev(other):
        return {"pts": other * NY + yc}

    def spread(buf, ssem, rsem, mine, other, device):
        return pltpu.make_async_remote_copy(
            src_ref=buf.at[mine],
            dst_ref=buf.at[mine],
            send_sem=ssem.at[other],
            recv_sem=rsem.at[mine],
            device_id=device,
            device_id_type=MESH,
        )

    def arrival(buf, ssem, rsem, other, device):
        return pltpu.make_async_remote_copy(
            src_ref=buf.at[other],
            dst_ref=buf.at[other],
            send_sem=ssem.at[other],
            recv_sem=rsem.at[other],
            device_id=device,
            device_id_type=MESH,
        )

    for d in far(NY):
        other = (yc + d) % NY
        spread(vy_ref, vy_s, vy_r, yc, other, y_dev(other)).start()

    for i in range(NC - 1):
        sender = freq_peer(i)
        gram_copy(sender, sender).wait_recv()
    gx_ref[...] = total_of(gr_ref, NC)

    def gram_y(other, slot):
        return pltpu.make_async_remote_copy(
            src_ref=gx_ref.at[pl.ds(pl.multiple_of(other * gsub, gsub), gsub), :],
            dst_ref=gy_ref.at[slot],
            send_sem=gy_s.at[other],
            recv_sem=gy_r.at[slot],
            device_id=y_dev(other),
            device_id_type=MESH,
        )

    for d in far(NY):
        gram_y((yc + d) % NY, yc).start()
    gy_ref[yc] = gx_ref[pl.ds(pl.multiple_of(yc * gsub, gsub), gsub), :]

    for d in far(NY):
        other = (yc + d) % NY
        arrival(vy_ref, vy_s, vy_r, other, y_dev(other)).wait_recv()
    vz_ref[zc] = total_of(vy_ref, NY)
    for d in far(nz):
        other = (zc + d) % nz
        spread(vz_ref, vz_s, vz_r, zc, other, z_dev(other)).start()

    for d in far(NY):
        other = (yc + d) % NY
        gram_y(other, other).wait_recv()
    gz_ref[zc] = total_of(gy_ref, NY)
    for d in far(nz):
        other = (zc + d) % nz
        spread(gz_ref, gz_s, gz_r, zc, other, z_dev(other)).start()

    for d in far(nz):
        other = (zc + d) % nz
        arrival(vz_ref, vz_s, vz_r, other, z_dev(other)).wait_recv()
    v = total_of(vz_ref, nz) * (1.0 / total_rows)

    square = v * v
    norm1 = jnp.sum(jnp.where(lane4 < 64, square, 0.0), axis=1, keepdims=True) * (1.0 / NB)
    norm2 = jnp.sum(jnp.where(lane4 >= 64, square, 0.0), axis=1, keepdims=True) * (1.0 / NB)
    y = v * (1.0 / jnp.sqrt(jnp.where(lane4 < 64, norm1, norm2) + 1e-06))
    turned = pltpu.roll(y, 64, 1)
    e_ref[me] = jnp.concatenate(
        [jnp.where(lane4 < 64, y, turned), jnp.where(lane4 < 64, turned, y)], axis=0
    )

    for i in range(NC - 1):
        to = freq_peer(i)
        spread(e_ref, e_s, e_r, me, to, {"freq": to}).start()

    line = lanes((2 * per, block), 0)
    own = lanes((2 * per, block)) // 64 == line % (per // 2) * 2 + line % per // (per // 2)
    sign = jnp.where(lanes((per, 128)) // 32 % 2 == 0, 1.0, -1.0)

    def project(slot):
        y = e_ref[order[slot]]
        e = jnp.concatenate([y * sign, pltpu.roll(y, 32, 1)], axis=0)
        left = jnp.where(own, jnp.concatenate([e] * (block // 128), axis=1), 0.0)
        high, low = split(left)
        first = slot * block
        right = ah_ref[first : first + block, :]
        both = dot(jnp.concatenate([high, low], axis=0), right)
        out = both[: 2 * per] + both[2 * per :] + dot(high, al_ref[first : first + block, :])
        return out * inv_root

    modes_out[me] = project(NC - 1)

    for d in far(nz):
        other = (zc + d) % nz
        arrival(gz_ref, gz_s, gz_r, other, z_dev(other)).wait_recv()
    gf_ref[yc] = total_of(gz_ref, nz) * (1.0 / total_rows)
    for d in far(NY):
        other = (yc + d) % NY
        spread(gf_ref, ga_s, ga_r, yc, other, y_dev(other)).start()

    def modes_copy(to, slot):
        return pltpu.make_async_remote_copy(
            src_ref=ms_ref.at[to],
            dst_ref=modes_out.at[slot],
            send_sem=m_s.at[to],
            recv_sem=m_r.at[slot],
            device_id={"freq": to},
            device_id_type=MESH,
        )

    for step in ((6,), (2, 3), (4, 5), (0, 1)):
        owners = [freq_peer(i) for i in step]
        for owner in owners:
            arrival(e_ref, e_s, e_r, owner, {"freq": owner}).wait_recv()
        values = [project(i) for i in step]
        for owner, value in zip(owners, values):
            ms_ref[owner] = value
        for owner in owners:
            modes_copy(owner, me).start()

    for d in far(NY):
        other = (yc + d) % NY
        arrival(gf_ref, ga_s, ga_r, other, y_dev(other)).wait_recv()
    for i in range(NY):
        gram_out[i * gsub : (i + 1) * gsub, :] = gf_ref[i]

    for i in range(NC - 1):
        to = freq_peer(i)
        gram_copy(to, me).wait_send()
        vx_copy(to, me).wait_send()
        spread(e_ref, e_s, e_r, me, to, {"freq": to}).wait_send()
    for d in far(NY):
        other = (yc + d) % NY
        spread(vy_ref, vy_s, vy_r, yc, other, y_dev(other)).wait_send()
        gram_y(other, yc).wait_send()
        spread(gf_ref, ga_s, ga_r, yc, other, y_dev(other)).wait_send()
    for d in far(nz):
        other = (zc + d) % nz
        spread(vz_ref, vz_s, vz_r, zc, other, z_dev(other)).wait_send()
        spread(gz_ref, gz_s, gz_r, zc, other, z_dev(other)).wait_send()

    for i in (6, 2, 3, 4, 5, 0, 1):
        sender = freq_peer(i)
        modes_copy(sender, sender).wait_recv()
    for i in range(NC - 1):
        modes_copy(freq_peer(i), me).wait_send()


def finish(gram_ref, modes_ref, gram_out, modes_out):
    rows = modes_ref.shape[2]
    per = modes_ref.shape[1] // 2
    for s in range(NC):
        value = modes_ref[s]
        for k in range(per):
            for c in range(2):
                line = c * per + k % 2 * (per // 2) + k // 2
                modes_out[k, c : c + 1, s * rows : (s + 1) * rows] = value[line : line + 1]
    packed = gram_ref[...]
    flipped = jnp.concatenate([packed, packed], axis=0).T
    above = lanes((NB, NB), 0) <= lanes((NB, NB))
    same = lanes((NB, NB), 0) == lanes((NB, NB))
    for q in range(per // 4):
        for k in range(4):
            here = packed[q * NB : (q + 1) * NB]
            there = flipped[k * NB : (k + 1) * NB]
            here = here if k == 0 else pltpu.roll(here, 128 - 32 * k, 1)
            there = there if q == 0 else pltpu.roll(there, 128 - 32 * q, 1)
            here, there = here[:, :NB], there[:, :NB]
            freq = 4 * q + (0, 2, 1, 3)[k]
            gram_out[freq, 0] = jnp.where(above, here, there)
            gram_out[freq, 1] = jnp.where(same, 0.0, jnp.where(above, -there, here))


def shards(nz, tables, snapshots, weight, start_vec):
    times, rows = snapshots.shape
    table, steady = tables
    total_rows = weight.shape[0] * lax.axis_size("pts")
    per = NF // NC
    dma = pltpu.SemaphoreType.DMA
    vmem = pl.BlockSpec(memory_space=pltpu.VMEM)
    gram_rows = per // 4 * NB
    gram, modes = pl.pallas_call(
        functools.partial(kernel, nz, total_rows, steady),
        out_shape=(
            jax.ShapeDtypeStruct((gram_rows, 128), F32),
            jax.ShapeDtypeStruct((NC, per * 2, rows), F32),
        ),
        in_specs=[pl.BlockSpec(memory_space=pltpu.HBM)] * 4,
        out_specs=(vmem, vmem),
        scratch_shapes=[
            pltpu.VMEM((weight.shape[0] // 128, 128), F32),
            pltpu.VMEM((2, NB, NF), F32),
            pltpu.VMEM(table.shape, BF),
            pltpu.VMEM((times, rows), F32),
            pltpu.VMEM((times * 2, rows), BF),
            pltpu.VMEM((rows // 128, NF * 2 * PITCH, 128), F32),
            pltpu.VMEM((NF * 2 * NB, rows), BF),
            pltpu.VMEM((NF * 2 * NB, rows), BF),
            pltpu.VMEM((NC, gram_rows, 128), F32),
            pltpu.VMEM((NC, gram_rows, 128), F32),
            pltpu.VMEM((NC, per // 2, 128), F32),
            pltpu.VMEM((NC, per // 2, 128), F32),
            pltpu.VMEM((gram_rows, 128), F32),
            pltpu.VMEM((NY, gram_rows // NY, 128), F32),
            pltpu.VMEM((nz, gram_rows // NY, 128), F32),
            pltpu.VMEM((NY, gram_rows // NY, 128), F32),
            pltpu.VMEM((NY, per // 2, 128), F32),
            pltpu.VMEM((nz, per // 2, 128), F32),
            pltpu.VMEM((NC, per, 128), F32),
            pltpu.VMEM((NC, per * 2, rows), F32),
            pltpu.VMEM((NF // 2, NB, 128), F32),
            pltpu.VMEM((NF // 2, NB, 128), F32),
            dma((3,)),
            dma((2,)),
            dma((NC,)),
            dma((NC,)),
            dma((NY,)),
            dma((NY,)),
            dma((nz,)),
            dma((nz,)),
            dma((NY,)),
            dma((NY,)),
            dma((NC,)),
            dma((NC,)),
            dma((NY,)),
            dma((NY,)),
            dma((nz,)),
            dma((nz,)),
            dma((NC,)),
            dma((NC,)),
            dma((NC,)),
            dma((NC,)),
        ],
        compiler_params=pltpu.CompilerParams(
            collective_id=0, has_side_effects=True, vmem_limit_bytes=40 * 1024 * 1024
        ),
        name="spod",
    )(
        *(
            pltpu.with_memory_space_constraint(a, pltpu.HBM)
            for a in (snapshots, weight.reshape(-1, 128), start_vec.transpose(1, 2, 0), jnp.asarray(table))
        )
    )
    return pl.pallas_call(
        finish,
        out_shape=(
            jax.ShapeDtypeStruct((per, 2, NB, NB), F32),
            jax.ShapeDtypeStruct((per, 2, NC * rows), F32),
        ),
        in_specs=[vmem, vmem],
        out_specs=(vmem, vmem),
        compiler_params=pltpu.CompilerParams(vmem_limit_bytes=16 * 1024 * 1024),
        name="finish",
    )(gram, modes)


def solution(mesh):
    placed = (P(None, ("pts", "freq")), P("pts"), P())
    nz = mesh.shape["pts"] // NY
    return jax.shard_map(
        functools.partial(shards, nz, dft_operand()),
        mesh=mesh,
        in_specs=placed,
        out_specs=(P("freq", None, None, None), P("freq", None, "pts")),
        check_vma=False,
    )
```
